128 devices in a mesh: tm: 16 (over x_hi, y, core), row: 2 (over x_lo), col: 4 (over z).
Axes of the slice: x: 4 (x_hi: 2, x_lo: 2; x = x_hi * 2 + x_lo), y: 4, z: 4, core: 2. Of those that a mesh axis runs over, the one named last changes fastest.
Arguments:
- coarse: bfloat16 [64, 16, 64, 256], P('tm', 'row', 'col'), may hold values from -6 to 6
- kernels: bfloat16 [3, 3, 3, 3, 256, 256], replicated, may hold values from -0.078125 to 0.078125
- biases: float32 [3, 256], replicated, may hold values from -3 to 3
Outputs:
- decoded: bfloat16 [64, 32, 128, 256], P('tm', 'row', 'col')
The draws below stay inside these ranges and needn't reach their ends.
All inputs are finite; a program needn't handle non-finite values.
Results may differ from the reference program's by a relative error of at most 0.0031.
Values may be sent and summed in bfloat16 or wider, within the bound.
A program may use at most 128 MiB of HBM per device.

```python
import jax
import jax.numpy as jnp
from jax import lax

C = 256
LAYERS = 3
FRAMES = 64
ROWS = 16
COLS = 64


def level_of(key, extent, pieces, low, high):
    loudness, own = 1.0, jax.random.fold_in(key, 6)
    for dim, parts in pieces:
        steps = jnp.exp(jax.random.uniform(jax.random.fold_in(own, dim), (parts,), jnp.float32, low / len(pieces), high / len(pieces)))
        loudness = loudness * jnp.repeat(steps, extent[dim] // parts).reshape([-1 if axis == dim else 1 for axis in range(len(extent))])
    return loudness


def bell_draw(own_key, shape, spread, bound, shards=(), kind=jnp.bfloat16):
    entries = jax.random.normal(own_key, shape, jnp.float32) * spread
    if len(shards) > 0:
        entries = level_of(own_key, shape, shards, -0.22, 0.18) * entries
    return jnp.clip(entries, min=-bound, max=bound).astype(kind)


def setup_inputs(seed: int = 0) -> dict:
    key_of = jax.random.split(jax.random.key(seed), 4)
    coarse = bell_draw(key_of[0], (FRAMES, ROWS, COLS, C), 1.0, 6.0, ((0, 16), (1, 2), (2, 4)))
    kernels = bell_draw(key_of[1], (LAYERS, 3, 3, 3, C, C), (27 * C) ** -0.5, 0.078125)
    biases = bell_draw(key_of[2], (LAYERS, C), 0.5, 3.0, (), jnp.float32)
    return {"coarse": coarse, "kernels": kernels, "biases": biases}


def upsample(values):
    return jnp.repeat(jnp.repeat(values, 2, axis=1), 2, axis=2)


def silu_round(values):
    return jax.nn.silu(values).astype(jnp.bfloat16)


def convolve(padded, kernel):
    frames = padded.shape[0] - 2
    height = padded.shape[1] - 2
    widths = padded.shape[2] - 2
    channels = kernel.shape[-1]

    def per_frame(frame_idx):
        window = lax.dynamic_slice_in_dim(padded, frame_idx.astype(jnp.int32), 3, 0)
        summed = jnp.zeros((height * widths, channels), jnp.float32)
        for t_off in range(3):
            for y_off in range(3):
                stacked = jnp.concatenate([window[t_off, y_off:y_off + height, x_off:x_off + widths] for x_off in range(3)], axis=-1)
                summed = summed + jnp.dot(stacked.reshape(-1, 3 * channels), kernel[t_off, y_off].reshape(3 * channels, channels), preferred_element_type=jnp.float32)
        return summed.reshape(height, widths, channels)

    return lax.map(per_frame, jnp.arange(frames).astype(jnp.int32))


def reference(coarse, kernels, biases):
    upsampled = upsample(coarse.astype(jnp.float32))
    acted = silu_round(upsampled)
    hidden = upsampled
    for layer_idx in range(LAYERS):
        padded = jnp.pad(acted, ((2, 0), (1, 1), (1, 1), (0, 0)))
        hidden = convolve(padded, kernels[layer_idx]) + biases[layer_idx]
        if layer_idx + 1 < LAYERS:
            acted = silu_round(hidden)
    return (upsampled + hidden).astype(jnp.bfloat16)
```

```python
import functools

import jax
import jax.numpy as jnp
from jax import lax
from jax.experimental import pallas as pl
from jax.experimental.pallas import tpu as pltpu
from jax.sharding import PartitionSpec as P

F32 = jnp.float32
BF16 = jnp.bfloat16
MESH = pl.DeviceIdType.MESH
C = 256
TAP = 9


def silu(v):
    return v * (0.5 + 0.5 * jnp.tanh(0.5 * v))


def joined(ref, *at):
    *outer, rows = at
    return jnp.concatenate([ref[(*outer, half, rows)] for half in range(2)], axis=-1)


def parted(value, ref, *at):
    *outer, rows = at
    for half in range(2):
        ref[(*outer, half, rows)] = value[:, 128 * half:128 * half + 128]


def rounded(v):
    return v.astype(BF16).astype(F32)


def kernel(sizes, coarse_hbm, kernels_hbm, bias_ref, out_hbm,
           wraw, u0, u1, raw, cells, cell_cols, cell_stage, diffs,
           act1, act2, cols1, cols2, stage1, stage2, v1, v2, acc, scr, oscr, obuf,
           in_sem, w_sem, out_sem, c_send, c_recv, h_send, h_recv):
    tms, rows, ncols = sizes
    tm, row, col = lax.axis_index("tm"), lax.axis_index("row"), lax.axis_index("col")
    other = 1 - row

    coarse_in = pltpu.make_async_copy(coarse_hbm, raw, in_sem)
    coarse_in.start()
    w_in = []
    for layer in range(3):
        for t in range(3):
            copy = pltpu.make_async_copy(
                kernels_hbm.at[layer, pl.ds(t * TAP, TAP)], wraw.at[layer, pl.ds(t * TAP, TAP)], w_sem.at[layer, t])
            copy.start()
            w_in.append(copy)

    cells[...] = jnp.zeros_like(cells)
    cell_cols[...] = jnp.zeros_like(cell_cols)
    cols1[...] = jnp.zeros_like(cols1)
    cols2[...] = jnp.zeros_like(cols2)
    for act in (act1, act2):
        edge = jnp.zeros((2, act.shape[1], 1, 16, C), BF16)
        act[:, :, 0:1] = edge
        act[:, :, 17:18] = edge

    peers = [(dt, dr, dc) for dt in range(3) for dr in range(2) for dc in (-1, 0, 1) if (dt, dr, dc) != (0, 0, 0)]

    def exists(dt, dc, sign):
        ok = True
        if dt:
            ok = (tm + sign * dt >= 0) & (tm + sign * dt < tms)
        if dc:
            near = (col + sign * dc >= 0) & (col + sign * dc < ncols)
            ok = near if ok is True else ok & near
        return ok

    def when(cond, body):
        if cond is True:
            body()
        else:
            pl.when(cond)(body)

    def place(dt, dr, dc, sign):
        return (tm + sign * dt, other if dr else row, col + sign * dc)

    barrier = pltpu.get_barrier_semaphore()
    for dt, dr, dc in peers:
        def greet(dt=dt, dr=dr, dc=dc):
            pl.semaphore_signal(barrier, inc=1, device_id=place(dt, dr, dc, -1), device_id_type=MESH)
        when(exists(dt, dc, -1), greet)

    coarse_in.wait()
    for f in range(4):
        acted = silu(raw[f].astype(F32)).astype(BF16)
        cells[6 + f, 1:9] = acted.reshape(8, 16, C)
        parted(acted.astype(F32), scr, 0, pl.ds(0, 128))
        cell_stage[0, f] = joined(scr, 0, pl.ds(15, 8, stride=16))
        cell_stage[1, f] = joined(scr, 0, pl.ds(0, 8, stride=16))

    ahead = jnp.minimum(tms - 1 - tm, 2)
    beside = jnp.minimum(col, 1) + jnp.minimum(ncols - 1 - col, 1)
    pl.semaphore_wait(barrier, (1 + ahead) * 2 * (1 + beside) - 1)

    groups = [(0, 0, 4, 6), (1, 2, 2, 4), (1, 0, 2, 2), (2, 2, 2, 0)]

    def cell_copy(g, kind):
        dt, src, count, dst = groups[g]
        if kind == 0:
            s, d, dr, dc = cells.at[pl.ds(6 + src, count), pl.ds(1, 8)], cells.at[pl.ds(dst, count), pl.ds(1, 8)], 0, 0
        elif kind == 1:
            s, d, dr, dc = cells.at[pl.ds(6 + src, count), 8 - 7 * row], cells.at[pl.ds(dst, count), 9 * row], 1, 0
        else:
            side = kind % 2
            dc = 1 - 2 * side
            if kind < 4:
                s, d, dr = cell_stage.at[side, pl.ds(src, count)], cell_cols.at[side, pl.ds(dst, count), pl.ds(8, 8)], 0
            else:
                at = pl.multiple_of(16 * row, 8)
                s, d, dr = cell_stage.at[side, pl.ds(src, count)], cell_cols.at[side, pl.ds(dst, count), pl.ds(at, 8)], 1
        copy = pltpu.make_async_remote_copy(
            src_ref=s, dst_ref=d, send_sem=c_send.at[g, kind], recv_sem=c_recv.at[g, kind],
            device_id=place(dt, dr, dc, 1), device_id_type=MESH)
        return copy, exists(dt, dc, 1), exists(dt, dc, -1)

    def cell_kinds(g):
        return range(1 if groups[g][0] == 0 else 0, 6)

    for g in range(4):
        for kind in cell_kinds(g):
            copy, there, _ = cell_copy(g, kind)
            when(there, copy.start)

    def cells_arrived(g):
        for kind in cell_kinds(g):
            copy, _, there = cell_copy(g, kind)
            when(there, copy.wait_recv)

    def halo_copy(layer, pair, kind):
        act, cols, stage = (act1, cols1, stage1) if layer == 1 else (act2, cols2, stage2)
        two = pl.ds(2 * pair, 2)
        if kind == 0:
            s, d, dr, dc = act.at[:, two, 16 - 15 * row], act.at[:, two, 17 * row], 1, 0
        else:
            side = (kind - 1) % 2
            dc = 1 - 2 * side
            if kind < 3:
                s, d, dr = stage.at[side, two], cols.at[side, two, pl.ds(8, 16)], 0
            else:
                s = stage.at[side, two, pl.ds(pl.multiple_of(8 * other, 8), 8)]
                d, dr = cols.at[side, two, pl.ds(pl.multiple_of(24 * row, 8), 8)], 1
        copy = pltpu.make_async_remote_copy(
            src_ref=s, dst_ref=d, send_sem=h_send.at[layer - 1, pair, kind], recv_sem=h_recv.at[layer - 1, pair, kind],
            device_id=place(0, dr, dc, 1), device_id_type=MESH)
        return copy, exists(0, dc, 1), exists(0, dc, -1)

    def send_halos(layer, pair):
        for kind in range(5):
            copy, there, _ = halo_copy(layer, pair, kind)
            when(there, copy.start)

    def halos_arrived(layer, pair):
        for kind in range(5):
            copy, _, there = halo_copy(layer, pair, kind)
            when(there, copy.wait_recv)

    def weights_0(t):
        w_in[t].wait()

        def chunk(i, carry):
            at = pl.ds(pl.multiple_of(i * 16, 16), 16)
            taps = [wraw[0, t * TAP + m, at, :].astype(F32) for m in range(9)]
            to = pl.ds(pl.multiple_of(t * C + i * 16, 16), 16)
            across = []
            for y in range(3):
                a, b, c = taps[3 * y:3 * y + 3]
                across.append([a, a + b + c, c])
            for kx in range(3):
                a, b, c = across[0][kx], across[1][kx], across[2][kx]
                for ky, value in enumerate((a, a + b + c, c)):
                    u0[ky * 3 + kx, to, :] = value.astype(BF16)
            return carry
        lax.fori_loop(0, 16, chunk, 0)

    def weights(layer):
        for t in range(3):
            w_in[3 * layer + t].wait()

        def chunk(i, carry):
            m, part = i // 4, i % 4
            at = pl.ds(pl.multiple_of(part * 64, 64), 64)
            to = pl.ds(pl.multiple_of(i * 64, 64), 64)
            a = wraw[layer, 3 * m, at, :]
            c = wraw[layer, 3 * m + 2, at, :]
            half = 0.5 * (a.astype(F32) + c.astype(F32))
            b = 0.5 * wraw[layer, 3 * m + 1, at, :].astype(F32)
            u1[layer - 1, 0, to, :] = a
            u1[layer - 1, 1, to, :] = (half + b).astype(BF16)
            u1[layer - 1, 2, to, :] = (half - b).astype(BF16)
            u1[layer - 1, 3, to, :] = c
            return carry
        lax.fori_loop(0, 36, chunk, 0)

    def build_diffs(first, count):
        def frame(f, carry):
            c = cells[f].astype(F32).reshape(160, C)
            every = pl.ds(0, 160)
            parted(pltpu.roll(c, 1, 0), scr, 0, every)
            parted(cell_cols[0, f, 7:17, :], scr, 0, pl.ds(0, 10, stride=16))
            parted(pltpu.roll(c, 159, 0), scr, 1, every)
            parted(cell_cols[1, f, 7:17, :], scr, 1, pl.ds(15, 10, stride=16))
            for kx, x in enumerate((joined(scr, 0, every) - c, c, joined(scr, 1, every) - c)):
                mid = x[16:144]
                diffs[kx, f] = (x[0:128] - mid).astype(BF16)
                diffs[3 + kx, f] = mid.astype(BF16)
                diffs[6 + kx, f] = (x[32:160] - mid).astype(BF16)
            return carry
        lax.fori_loop(first, first + count, frame, 0)

    live = tm > 0

    def layer_0(pair):
        o = 2 * pair
        for m in range(9):
            lhs = jnp.concatenate([diffs[m, o + t:o + t + 2].reshape(256, C) for t in range(3)], axis=1)
            parted(jnp.dot(lhs, u0[m], preferred_element_type=F32), acc, m, pl.ds(0, 256))
        bias = bias_ref[0:1, :]

        def phases(at):
            p = [joined(acc, m, at) for m in range(9)]
            left, right = p[4] + p[3] + bias, p[4] + p[5] + bias
            out = [[left + (p[1] + p[0]), right + (p[1] + p[2])],
                   [left + (p[7] + p[6]), right + (p[7] + p[8])]]
            out = [[silu(v) for v in line] for line in out]
            if pair < 2:
                out = [[jnp.where(live, v, 0.0) for v in line] for line in out]
            return out

        for side, x in ((0, 15), (1, 0)):
            edge = phases(pl.ds(x, 16, stride=16))
            for py in range(2):
                parted(rounded(edge[py][1 - side]), scr, 0, pl.ds(py, 16, stride=2))
            for f in range(2):
                stage1[side, o + f] = joined(scr, 0, pl.ds(16 * f, 16))
        for f in range(2):
            def line(i, carry, f=f):
                out = phases(pl.ds(pl.multiple_of(f * 128 + i * 16, 16), 16))
                for py in range(2):
                    for px in range(2):
                        act1[px, o + f, 1 + 2 * i + py] = out[py][px].astype(BF16)
                return carry
            lax.fori_loop(0, 8, line, 0, unroll=2)
        send_halos(1, pair)

    def build_v(layer, pair):
        act, cols, v = (act1, cols1, v1) if layer == 1 else (act2, cols2, v2)
        halos_arrived(layer, pair)
        for f in (2 * pair, 2 * pair + 1):
            e = act[0, f].astype(F32).reshape(288, C)
            o = act[1, f].astype(F32).reshape(288, C)
            every = pl.ds(0, 288)
            parted(pltpu.roll(o, 1, 0), scr, 0, every)
            parted(cols[0, f, 7:25, :], scr, 0, pl.ds(0, 18, stride=16))
            parted(pltpu.roll(e, 287, 0), scr, 1, every)
            parted(cols[1, f, 7:25, :], scr, 1, pl.ds(15, 18, stride=16))
            v[0, f] = (joined(scr, 0, every) - o).astype(BF16)
            v[1, f] = (e + o).astype(BF16)
            v[2, f] = (o - e).astype(BF16)
            v[3, f] = (e - joined(scr, 1, every)).astype(BF16)

    def products(layer, pair):
        v = v1 if layer == 1 else v2
        o = 2 * pair
        for k in range(4):
            lhs = jnp.concatenate(
                [v[k, o + t:o + t + 2, 16 * y:16 * y + 256].reshape(512, C) for t in range(3) for y in range(3)], axis=1)
            parted(jnp.dot(lhs, u1[layer - 1, k], preferred_element_type=F32), acc, k, pl.ds(0, 512))

    def outputs(layer, at):
        bias = bias_ref[layer:layer + 1, :]
        m = [joined(acc, k, at) for k in range(4)]
        return (m[0] + m[1]) + (m[2] + bias), (m[1] - m[2]) - (m[3] - bias)

    def layer_1(pair):
        products(1, pair)
        o = 2 * pair

        def acted(at):
            out = [silu(v) for v in outputs(1, at)]
            if pair < 1:
                out = [jnp.where(live, v, 0.0) for v in out]
            return out

        for side, x in ((0, 15), (1, 0)):
            value = rounded(acted(pl.ds(x, 32, stride=16))[1 - side])
            for f in range(2):
                stage2[side, o + f] = value[16 * f:16 * f + 16]
        for f in range(2):
            def line(i, carry, f=f):
                e, o_ = acted(pl.ds(pl.multiple_of(f * 256 + i * 32, 32), 32))
                two = pl.ds(1 + 2 * i, 2)
                act2[0, o + f, two] = e.astype(BF16).reshape(2, 16, C)
                act2[1, o + f, two] = o_.astype(BF16).reshape(2, 16, C)
                return carry
            lax.fori_loop(0, 8, line, 0, unroll=2)
        send_halos(2, pair)

    def layer_2(pair):
        products(2, pair)
        for f in range(2):
            def line(i, carry, f=f):
                e, o_ = outputs(2, pl.ds(pl.multiple_of(f * 256 + i * 32, 32), 32))
                up = raw[2 * pair + f, pl.ds(pl.multiple_of(i * 16, 16), 16), :].astype(F32)
                up = jnp.concatenate([up, up], axis=0)
                for lane in range(2):
                    half = slice(128 * lane, 128 * lane + 128)
                    oscr[lane, pl.ds(0, 32, stride=2), :] = (up + e)[:, half]
                    oscr[lane, pl.ds(1, 32, stride=2), :] = (up + o_)[:, half]
                    obuf[2 * pair + f, pl.ds(pl.multiple_of(i * 64, 64), 64), half] = oscr[lane].astype(BF16)
                return carry
            lax.fori_loop(0, 8, line, 0)
        copy = pltpu.make_async_copy(
            obuf.at[pl.ds(2 * pair, 2)], out_hbm.at[pl.ds(2 * pair, 2)], out_sem.at[pair])
        copy.start()
        return copy

    for t in range(3):
        weights_0(t)
    cells_arrived(0)
    build_diffs(6, 4)
    layer_0(3)
    weights(1)
    cells_arrived(1)
    build_diffs(4, 2)
    layer_0(2)
    cells_arrived(2)
    build_diffs(2, 2)
    layer_0(1)
    build_v(1, 3)
    build_v(1, 2)
    layer_1(2)
    cells_arrived(3)
    build_diffs(0, 2)
    layer_0(0)
    weights(2)
    build_v(1, 1)
    layer_1(1)
    build_v(1, 0)
    layer_1(0)
    build_v(2, 2)
    build_v(2, 1)
    out_b = layer_2(1)
    build_v(2, 0)
    out_a = layer_2(0)
    out_b.wait()
    out_a.wait()

    for g in range(4):
        for kind in cell_kinds(g):
            copy, there, _ = cell_copy(g, kind)
            when(there, copy.wait_send)
    for layer, pairs in ((1, 4), (2, 3)):
        for pair in range(pairs):
            for kind in range(5):
                copy, there, _ = halo_copy(layer, pair, kind)
                when(there, copy.wait_send)


def solution(mesh):
    sizes = tuple(mesh.shape[name] for name in ("tm", "row", "col"))

    def local(coarse, kernels, biases):
        any_space = pl.BlockSpec(memory_space=pl.ANY)
        decoded = pl.pallas_call(
            functools.partial(kernel, sizes),
            out_shape=jax.ShapeDtypeStruct((4, 512, C), BF16),
            in_specs=[any_space, any_space, pl.BlockSpec(memory_space=pltpu.VMEM)],
            out_specs=any_space,
            scratch_shapes=[
                pltpu.VMEM((3, 27, C, C), BF16),
                pltpu.VMEM((9, 3 * C, C), BF16),
                pltpu.VMEM((2, 4, 9 * C, C), BF16),
                pltpu.VMEM((4, 128, C), BF16),
                pltpu.VMEM((10, 10, 16, C), BF16),
                pltpu.VMEM((2, 10, 24, C), F32),
                pltpu.VMEM((2, 4, 8, C), F32),
                pltpu.VMEM((9, 10, 128, C), BF16),
                pltpu.VMEM((2, 8, 18, 16, C), BF16),
                pltpu.VMEM((2, 6, 18, 16, C), BF16),
                pltpu.VMEM((2, 8, 32, C), F32),
                pltpu.VMEM((2, 6, 32, C), F32),
                pltpu.VMEM((2, 8, 16, C), F32),
                pltpu.VMEM((2, 6, 16, C), F32),
                pltpu.VMEM((4, 8, 288, C), BF16),
                pltpu.VMEM((4, 6, 288, C), BF16),
                pltpu.VMEM((9, 2, 512, 128), F32),
                pltpu.VMEM((2, 2, 288, 128), F32),
                pltpu.VMEM((2, 64, 128), F32),
                pltpu.VMEM((4, 512, C), BF16),
                pltpu.SemaphoreType.DMA,
                pltpu.SemaphoreType.DMA((3, 3)),
                pltpu.SemaphoreType.DMA((2,)),
                pltpu.SemaphoreType.DMA((4, 6)),
                pltpu.SemaphoreType.DMA((4, 6)),
                pltpu.SemaphoreType.DMA((2, 4, 5)),
                pltpu.SemaphoreType.DMA((2, 4, 5)),
            ],
            compiler_params=pltpu.CompilerParams(
                collective_id=0, has_side_effects=True, vmem_limit_bytes=62 * 2**20),
        )(coarse.reshape(4, 128, C), kernels.reshape(3, 27, C, C), biases)
        return decoded.reshape(4, 16, 32, C)

    return jax.shard_map(
        local, mesh=mesh, in_specs=(P("tm", "row", "col", None), P(), P()),
        out_specs=P("tm", "row", "col", None), check_vma=False)
```

```python
import functools

import jax
import jax.numpy as jnp
from jax import lax
from jax.experimental import pallas as pl
from jax.experimental.pallas import tpu as pltpu
from jax.sharding import PartitionSpec as P

F32 = jnp.float32
BF16 = jnp.bfloat16
MESH = pl.DeviceIdType.MESH
C = 256
TAP = 9


def silu(v):
    return v * (0.5 + 0.5 * jnp.tanh(0.5 * v))


def joined(ref, *at):
    *outer, rows = at
    return jnp.concatenate([ref[(*outer, half, rows)] for half in range(2)], axis=-1)


def parted(value, ref, *at):
    *outer, rows = at
    for half in range(2):
        ref[(*outer, half, rows)] = value[:, 128 * half:128 * half + 128]


def rounded(v):
    return v.astype(BF16).astype(F32)


def kernel(sizes, coarse_hbm, kernels_hbm, bias_ref, obuf,
           wraw, u0, u1, raw, cells, cell_cols, cell_ends, cell_stage, cell_tips, diffs,
           act1, act2, cols1, cols2, ends1, ends2, stage1, stage2, tips1, tips2, v1, v2, acc, scr, oscr,
           in_sem, w_sem, c_send, c_recv, h_send, h_recv):
    tms, rows, ncols = sizes
    tm, row, col = lax.axis_index("tm"), lax.axis_index("row"), lax.axis_index("col")
    other = 1 - row

    coarse_in = pltpu.make_async_copy(coarse_hbm, raw, in_sem)
    coarse_in.start()
    w_in = []
    for layer in range(3):
        for t in range(3):
            copy = pltpu.make_async_copy(
                kernels_hbm.at[layer, pl.ds(t * TAP, TAP)], wraw.at[layer, pl.ds(t * TAP, TAP)], w_sem.at[layer, t])
            w_in.append(copy)
    for copy in w_in[:3]:
        copy.start()

    peers = [(dt, dr, dc) for dt in range(3) for dr in range(2) for dc in (-1, 0, 1) if (dt, dr, dc) != (0, 0, 0)]

    def exists(dt, dc, sign):
        ok = True
        if dt:
            ok = (tm + sign * dt >= 0) & (tm + sign * dt < tms)
        if dc:
            near = (col + sign * dc >= 0) & (col + sign * dc < ncols)
            ok = near if ok is True else ok & near
        return ok

    def when(cond, body):
        if cond is True:
            body()
        else:
            pl.when(cond)(body)

    def place(dt, dr, dc, sign):
        return (tm + sign * dt, other if dr else row, col + sign * dc)

    barrier = pltpu.get_barrier_semaphore()
    for dt, dr, dc in peers:
        def greet(dt=dt, dr=dr, dc=dc):
            pl.semaphore_signal(barrier, inc=1, device_id=place(dt, dr, dc, -1), device_id_type=MESH)
        when(exists(dt, dc, -1), greet)

    def clear(*refs):
        for ref in refs:
            ref[...] = jnp.zeros(ref.shape, ref.dtype)

    clear(cells.at[:, 9 * row], act1.at[:, :, 17 * row], act2.at[:, :, 17 * row])
    for side, edge in ((0, 0), (1, ncols - 1)):
        @pl.when(col == edge)
        def _(side=side):
            clear(*(ref.at[side] for ref in (cell_cols, cell_ends, cols1, cols2, ends1, ends2)))

    def clear_frames(first, count):
        at = pl.ds(first, count)
        clear(cells.at[at], cell_cols.at[:, at], cell_ends.at[:, at])

    @pl.when(tm < 2)
    def _():
        clear_frames(0, 2)

    @pl.when(tm < 1)
    def _():
        clear_frames(2, 4)

    coarse_in.wait()
    for f in range(4):
        acted = silu(raw[f].astype(F32)).astype(BF16)
        cells[6 + f, 1:9] = acted.reshape(8, 16, C)
        parted(acted.astype(F32), scr, 0, pl.ds(0, 128))
        for side, x in ((0, 15), (1, 0)):
            edge = joined(scr, 0, pl.ds(x, 8, stride=16))
            cell_stage[side, f] = edge.astype(BF16)
            cell_tips[side, f] = jnp.where(row == 0, edge[7:8], edge[0:1])

    def weights_0(t):
        w_in[t].wait()

        def chunk(i, carry):
            at = pl.ds(pl.multiple_of(i * 16, 16), 16)
            taps = [wraw[0, t * TAP + m, at, :].astype(F32) for m in range(9)]
            to = pl.ds(pl.multiple_of(t * C + i * 16, 16), 16)
            across = []
            for y in range(3):
                a, b, c = taps[3 * y:3 * y + 3]
                across.append([a, a + b + c, c])
            for kx in range(3):
                a, b, c = across[0][kx], across[1][kx], across[2][kx]
                for ky, value in enumerate((a, a + b + c, c)):
                    u0[ky * 3 + kx, to, :] = value.astype(BF16)
            return carry
        lax.fori_loop(0, 16, chunk, 0)

    def weights(layer):
        for t in range(3):
            w_in[3 * layer + t].wait()

        def chunk(i, carry):
            m, part = i // 4, i % 4
            at = pl.ds(pl.multiple_of(part * 64, 64), 64)
            to = pl.ds(pl.multiple_of(i * 64, 64), 64)
            a = wraw[layer, 3 * m, at, :]
            c = wraw[layer, 3 * m + 2, at, :]
            half = 0.5 * (a.astype(F32) + c.astype(F32))
            b = 0.5 * wraw[layer, 3 * m + 1, at, :].astype(F32)
            u1[layer - 1, 0, to, :] = a
            u1[layer - 1, 1, to, :] = (half + b).astype(BF16)
            u1[layer - 1, 2, to, :] = (half - b).astype(BF16)
            u1[layer - 1, 3, to, :] = c
            return carry
        lax.fori_loop(0, 36, chunk, 0)

    for t in range(3):
        weights_0(t)

    ahead = jnp.minimum(tms - 1 - tm, 2)
    beside = jnp.minimum(col, 1) + jnp.minimum(ncols - 1 - col, 1)
    pl.semaphore_wait(barrier, (1 + ahead) * 2 * (1 + beside) - 1)

    groups = [(0, 0, 4, 6), (1, 2, 2, 4), (1, 0, 2, 2), (2, 2, 2, 0)]

    def cell_copy(g, kind):
        dt, src, count, dst = groups[g]
        if kind == 0:
            s, d, dr, dc = cells.at[pl.ds(6 + src, count), pl.ds(1, 8)], cells.at[pl.ds(dst, count), pl.ds(1, 8)], 0, 0
        elif kind == 1:
            s, d, dr, dc = cells.at[pl.ds(6 + src, count), 8 - 7 * row], cells.at[pl.ds(dst, count), 9 * row], 1, 0
        else:
            side = kind % 2
            dc = 1 - 2 * side
            if kind < 4:
                s, d, dr = cell_stage.at[side, pl.ds(src, count)], cell_cols.at[side, pl.ds(dst, count)], 0
            else:
                s, d, dr = cell_tips.at[side, pl.ds(src, count)], cell_ends.at[side, pl.ds(dst, count)], 1
        copy = pltpu.make_async_remote_copy(
            src_ref=s, dst_ref=d, send_sem=c_send.at[g, kind], recv_sem=c_recv.at[g, kind],
            device_id=place(dt, dr, dc, 1), device_id_type=MESH)
        return copy, exists(dt, dc, 1), exists(dt, dc, -1)

    def cell_kinds(g):
        return range(1 if groups[g][0] == 0 else 0, 6)

    for g in range(4):
        for kind in cell_kinds(g):
            copy, there, _ = cell_copy(g, kind)
            when(there, copy.start)

    for copy in w_in[3:]:
        copy.start()

    def cells_arrived(g):
        for kind in cell_kinds(g):
            copy, _, there = cell_copy(g, kind)
            when(there, copy.wait_recv)

    fine = {1: (act1, cols1, ends1, stage1, tips1), 2: (act2, cols2, ends2, stage2, tips2)}

    def halo_copy(layer, pair, kind):
        act, cols, ends, stage, tips = fine[layer]
        two = pl.ds(2 * pair, 2)
        if kind == 0:
            s, d, dr, dc = act.at[:, two, 16 - 15 * row], act.at[:, two, 17 * row], 1, 0
        else:
            side = (kind - 1) % 2
            dc = 1 - 2 * side
            if kind < 3:
                s, d, dr = stage.at[side, two], cols.at[side, two], 0
            else:
                s, d, dr = tips.at[side, two], ends.at[side, two], 1
        copy = pltpu.make_async_remote_copy(
            src_ref=s, dst_ref=d, send_sem=h_send.at[layer - 1, pair, kind], recv_sem=h_recv.at[layer - 1, pair, kind],
            device_id=place(0, dr, dc, 1), device_id_type=MESH)
        return copy, exists(0, dc, 1), exists(0, dc, -1)

    def send_halos(layer, pair):
        for kind in range(5):
            copy, there, _ = halo_copy(layer, pair, kind)
            when(there, copy.start)

    def halos_arrived(layer, pair):
        for kind in range(5):
            copy, _, there = halo_copy(layer, pair, kind)
            when(there, copy.wait_recv)

    def put_edge(n, first, cols, ends, side, f):
        height = cols.shape[2]
        parted(cols[side, f].astype(F32), scr, n, pl.ds(first + 16, height, stride=16))
        end = ends[side, f]
        parted(jnp.where(row == 1, end, 0.0), scr, n, pl.ds(first, 1))
        parted(jnp.where(row == 0, end, 0.0), scr, n, pl.ds(first + 16 * height + 16, 1))

    def build_diffs(first, count):
        def frame(f, carry):
            c = cells[f].astype(F32).reshape(160, C)
            every = pl.ds(0, 160)
            parted(pltpu.roll(c, 1, 0), scr, 0, every)
            put_edge(0, 0, cell_cols, cell_ends, 0, f)
            parted(pltpu.roll(c, 159, 0), scr, 1, every)
            put_edge(1, 15, cell_cols, cell_ends, 1, f)
            for kx, x in enumerate((joined(scr, 0, every) - c, c, joined(scr, 1, every) - c)):
                mid = x[16:144]
                diffs[kx, f] = (x[0:128] - mid).astype(BF16)
                diffs[3 + kx, f] = mid.astype(BF16)
                diffs[6 + kx, f] = (x[32:160] - mid).astype(BF16)
            return carry
        lax.fori_loop(first, first + count, frame, 0)

    live = tm > 0

    def layer_0(pair):
        o = 2 * pair
        for m in range(9):
            lhs = jnp.concatenate([diffs[m, o + t:o + t + 2].reshape(256, C) for t in range(3)], axis=1)
            parted(jnp.dot(lhs, u0[m], preferred_element_type=F32), acc, m, pl.ds(0, 256))
        bias = bias_ref[0:1, :]

        def phases(at):
            p = [joined(acc, m, at) for m in range(9)]
            left, right = p[4] + p[3] + bias, p[4] + p[5] + bias
            out = [[left + (p[1] + p[0]), right + (p[1] + p[2])],
                   [left + (p[7] + p[6]), right + (p[7] + p[8])]]
            out = [[silu(v) for v in line] for line in out]
            if pair < 2:
                out = [[jnp.where(live, v, 0.0) for v in line] for line in out]
            return out

        for side, x in ((0, 15), (1, 0)):
            edge = phases(pl.ds(x, 16, stride=16))
            for py in range(2):
                parted(rounded(edge[py][1 - side]), scr, 0, pl.ds(py, 16, stride=2))
            for f in range(2):
                value = joined(scr, 0, pl.ds(16 * f, 16))
                stage1[side, o + f] = value.astype(BF16)
                tips1[side, o + f] = jnp.where(row == 0, value[15:16], value[0:1])
        for f in range(2):
            def line(i, carry, f=f):
                out = phases(pl.ds(pl.multiple_of(f * 128 + i * 16, 16), 16))
                for py in range(2):
                    for px in range(2):
                        act1[px, o + f, 1 + 2 * i + py] = out[py][px].astype(BF16)
                return carry
            lax.fori_loop(0, 8, line, 0, unroll=2)
        send_halos(1, pair)

    def build_v(layer, pair):
        act, cols, ends, _, _ = fine[layer]
        v = v1 if layer == 1 else v2
        halos_arrived(layer, pair)
        for f in (2 * pair, 2 * pair + 1):
            e = act[0, f].astype(F32).reshape(288, C)
            o = act[1, f].astype(F32).reshape(288, C)
            every = pl.ds(0, 288)
            parted(pltpu.roll(o, 1, 0), scr, 0, every)
            put_edge(0, 0, cols, ends, 0, f)
            parted(pltpu.roll(e, 287, 0), scr, 1, every)
            put_edge(1, 15, cols, ends, 1, f)
            v[0, f] = (joined(scr, 0, every) - o).astype(BF16)
            v[1, f] = (e + o).astype(BF16)
            v[2, f] = (o - e).astype(BF16)
            v[3, f] = (e - joined(scr, 1, every)).astype(BF16)

    def products(layer, pair):
        v = v1 if layer == 1 else v2
        o = 2 * pair
        for k in range(4):
            lhs = jnp.concatenate(
                [v[k, o + t:o + t + 2, 16 * y:16 * y + 256].reshape(512, C) for t in range(3) for y in range(3)], axis=1)
            parted(jnp.dot(lhs, u1[layer - 1, k], preferred_element_type=F32), acc, k, pl.ds(0, 512))

    def outputs(layer, at):
        bias = bias_ref[layer:layer + 1, :]
        m = [joined(acc, k, at) for k in range(4)]
        return (m[0] + m[1]) + (m[2] + bias), (m[1] - m[2]) - (m[3] - bias)

    def layer_1(pair):
        products(1, pair)
        o = 2 * pair

        def acted(at):
            out = [silu(v) for v in outputs(1, at)]
            if pair < 1:
                out = [jnp.where(live, v, 0.0) for v in out]
            return out

        for side, x in ((0, 15), (1, 0)):
            value = rounded(acted(pl.ds(x, 32, stride=16))[1 - side])
            for f in range(2):
                line = value[16 * f:16 * f + 16]
                stage2[side, o + f] = line.astype(BF16)
                tips2[side, o + f] = jnp.where(row == 0, line[15:16], line[0:1])
        for f in range(2):
            def line(i, carry, f=f):
                e, o_ = acted(pl.ds(pl.multiple_of(f * 256 + i * 32, 32), 32))
                two = pl.ds(1 + 2 * i, 2)
                act2[0, o + f, two] = e.astype(BF16).reshape(2, 16, C)
                act2[1, o + f, two] = o_.astype(BF16).reshape(2, 16, C)
                return carry
            lax.fori_loop(0, 8, line, 0, unroll=2)
        send_halos(2, pair)

    def layer_2(pair):
        products(2, pair)
        for f in range(2):
            def line(i, carry, f=f):
                e, o_ = outputs(2, pl.ds(pl.multiple_of(f * 256 + i * 32, 32), 32))
                up = raw[2 * pair + f, pl.ds(pl.multiple_of(i * 16, 16), 16), :].astype(F32)
                up = jnp.concatenate([up, up], axis=0)
                for lane in range(2):
                    half = slice(128 * lane, 128 * lane + 128)
                    oscr[lane, pl.ds(0, 32, stride=2), :] = (up + e)[:, half]
                    oscr[lane, pl.ds(1, 32, stride=2), :] = (up + o_)[:, half]
                    obuf[2 * pair + f, pl.ds(pl.multiple_of(i * 64, 64), 64), half] = oscr[lane].astype(BF16)
                return carry
            lax.fori_loop(0, 8, line, 0)

    weights(1)
    weights(2)
    cells_arrived(0)
    build_diffs(6, 4)
    layer_0(3)
    cells_arrived(1)
    build_diffs(4, 2)
    layer_0(2)
    cells_arrived(2)
    build_diffs(2, 2)
    layer_0(1)
    build_v(1, 3)
    build_v(1, 2)
    layer_1(2)
    cells_arrived(3)
    build_diffs(0, 2)
    layer_0(0)
    build_v(1, 1)
    layer_1(1)
    build_v(1, 0)
    layer_1(0)
    build_v(2, 2)
    build_v(2, 1)
    layer_2(1)
    build_v(2, 0)
    layer_2(0)

    for g in range(4):
        for kind in cell_kinds(g):
            copy, there, _ = cell_copy(g, kind)
            when(there, copy.wait_send)
    for layer, pairs in ((1, 4), (2, 3)):
        for pair in range(pairs):
            for kind in range(5):
                copy, there, _ = halo_copy(layer, pair, kind)
                when(there, copy.wait_send)


def solution(mesh):
    sizes = tuple(mesh.shape[name] for name in ("tm", "row", "col"))

    def local(coarse, kernels, biases):
        any_space = pl.BlockSpec(memory_space=pl.ANY)
        decoded = pl.pallas_call(
            functools.partial(kernel, sizes),
            out_shape=pltpu.VMEM((4, 512, C), BF16),
            in_specs=[any_space, any_space, pl.BlockSpec(memory_space=pltpu.VMEM)],
            out_specs=pl.BlockSpec(memory_space=pltpu.VMEM),
            scratch_shapes=[
                pltpu.VMEM((3, 27, C, C), BF16),
                pltpu.VMEM((9, 3 * C, C), BF16),
                pltpu.VMEM((2, 4, 9 * C, C), BF16),
                pltpu.VMEM((4, 128, C), BF16),
                pltpu.VMEM((10, 10, 16, C), BF16),
                pltpu.VMEM((2, 10, 8, C), BF16),
                pltpu.VMEM((2, 10, 1, C), F32),
                pltpu.VMEM((2, 4, 8, C), BF16),
                pltpu.VMEM((2, 4, 1, C), F32),
                pltpu.VMEM((9, 10, 128, C), BF16),
                pltpu.VMEM((2, 8, 18, 16, C), BF16),
                pltpu.VMEM((2, 6, 18, 16, C), BF16),
                pltpu.VMEM((2, 8, 16, C), BF16),
                pltpu.VMEM((2, 6, 16, C), BF16),
                pltpu.VMEM((2, 8, 1, C), F32),
                pltpu.VMEM((2, 6, 1, C), F32),
                pltpu.VMEM((2, 8, 16, C), BF16),
                pltpu.VMEM((2, 6, 16, C), BF16),
                pltpu.VMEM((2, 8, 1, C), F32),
                pltpu.VMEM((2, 6, 1, C), F32),
                pltpu.VMEM((4, 8, 288, C), BF16),
                pltpu.VMEM((4, 6, 288, C), BF16),
                pltpu.VMEM((9, 2, 512, 128), F32),
                pltpu.VMEM((2, 2, 288, 128), F32),
                pltpu.VMEM((2, 64, 128), F32),
                pltpu.SemaphoreType.DMA,
                pltpu.SemaphoreType.DMA((3, 3)),
                pltpu.SemaphoreType.DMA((4, 6)),
                pltpu.SemaphoreType.DMA((4, 6)),
                pltpu.SemaphoreType.DMA((2, 4, 5)),
                pltpu.SemaphoreType.DMA((2, 4, 5)),
            ],
            compiler_params=pltpu.CompilerParams(
                collective_id=0, has_side_effects=True, vmem_limit_bytes=56 * 2**20),
        )(coarse.reshape(4, 128, C), kernels.reshape(3, 27, C, C), biases)
        return decoded.reshape(4, 16, 32, C)

    return jax.shard_map(
        local, mesh=mesh, in_specs=(P("tm", "row", "col", None), P(), P()),
        out_specs=P("tm", "row", "col", None), check_vma=False)
```

```python
import functools

import jax
import jax.numpy as jnp
from jax import lax
from jax.experimental import pallas as pl
from jax.experimental.pallas import tpu as pltpu
from jax.sharding import PartitionSpec as P

F32 = jnp.float32
BF16 = jnp.bfloat16
MESH = pl.DeviceIdType.MESH
C = 256
TAP = 9


def silu(v):
    return v * (0.5 + 0.5 * jnp.tanh(0.5 * v))


def joined(ref, *at):
    *outer, rows = at
    return jnp.concatenate([ref[(*outer, half, rows)] for half in range(2)], axis=-1)


def parted(value, ref, *at):
    *outer, rows = at
    for half in range(2):
        ref[(*outer, half, rows)] = value[:, 128 * half:128 * half + 128]


def rounded(v):
    return v.astype(BF16).astype(F32)


def kernel(sizes, coarse_hbm, kernels_hbm, bias_ref, obuf,
           wraw, u0, u1, raw, cells, cell_cols, cell_ends, cell_stage, cell_tips, diffs,
           act1, act2, cols1, cols2, ends1, ends2, stage1, stage2, tips1, tips2, v1, v2, acc, scr, oscr,
           in_sem, w_sem, c_send, c_recv, h_send, h_recv):
    tms, rows, ncols = sizes
    tm, row, col = lax.axis_index("tm"), lax.axis_index("row"), lax.axis_index("col")
    other = 1 - row

    coarse_in = pltpu.make_async_copy(coarse_hbm, raw, in_sem)
    coarse_in.start()
    w_in = []
    for layer in range(3):
        for t in range(3):
            copy = pltpu.make_async_copy(
                kernels_hbm.at[layer, pl.ds(t * TAP, TAP)], wraw.at[layer, pl.ds(t * TAP, TAP)], w_sem.at[layer, t])
            w_in.append(copy)
    for copy in w_in[:3]:
        copy.start()

    peers = [(dt, dr, dc) for dt in range(2) for dr in range(2) for dc in (-1, 0, 1) if (dt, dr, dc) != (0, 0, 0)]

    def exists(dt, dc, sign):
        ok = True
        if dt:
            ok = (tm + sign * dt >= 0) & (tm + sign * dt < tms)
        if dc:
            near = (col + sign * dc >= 0) & (col + sign * dc < ncols)
            ok = near if ok is True else ok & near
        return ok

    def when(cond, body):
        if cond is True:
            body()
        else:
            pl.when(cond)(body)

    def place(dt, dr, dc, sign):
        return (tm + sign * dt, other if dr else row, col + sign * dc)

    barrier = pltpu.get_barrier_semaphore()
    for dt, dr, dc in peers:
        def greet(dt=dt, dr=dr, dc=dc):
            pl.semaphore_signal(barrier, inc=1, device_id=place(dt, dr, dc, -1), device_id_type=MESH)
        when(exists(dt, dc, -1), greet)

    def clear(*refs):
        for ref in refs:
            ref[...] = jnp.zeros(ref.shape, ref.dtype)

    clear(cells.at[:, 9 * row], act1.at[:, :, 17 * row], act2.at[:, :, 17 * row])
    for side, edge in ((0, 0), (1, ncols - 1)):
        @pl.when(col == edge)
        def _(side=side):
            clear(*(ref.at[side] for ref in (cell_cols, cell_ends, cols1, cols2, ends1, ends2)))

    def clear_frames(first, count):
        at = pl.ds(first, count)
        clear(cells.at[at], cell_cols.at[:, at], cell_ends.at[:, at])

    @pl.when(tm < 1)
    def _():
        clear_frames(0, 4)
        clear(act2.at[:, 0:2], cols2.at[:, 0:2], ends2.at[:, 0:2])

    coarse_in.wait()
    for f in range(4):
        acted = silu(raw[f].astype(F32)).astype(BF16)
        cells[4 + f, 1:9] = acted.reshape(8, 16, C)
        parted(acted.astype(F32), scr, 0, pl.ds(0, 128))
        for side, x in ((0, 15), (1, 0)):
            edge = joined(scr, 0, pl.ds(x, 8, stride=16))
            cell_stage[side, f] = edge.astype(BF16)
            cell_tips[side, f] = jnp.where(row == 0, edge[7:8], edge[0:1])

    def weights_0(t):
        w_in[t].wait()

        def chunk(i, carry):
            at = pl.ds(pl.multiple_of(i * 16, 16), 16)
            taps = [wraw[0, t * TAP + m, at, :].astype(F32) for m in range(9)]
            to = pl.ds(pl.multiple_of(t * C + i * 16, 16), 16)
            across = []
            for y in range(3):
                a, b, c = taps[3 * y:3 * y + 3]
                across.append([a, a + b + c, c])
            for kx in range(3):
                a, b, c = across[0][kx], across[1][kx], across[2][kx]
                for ky, value in enumerate((a, a + b + c, c)):
                    u0[ky * 3 + kx, to, :] = value.astype(BF16)
            return carry
        lax.fori_loop(0, 16, chunk, 0)

    def weights(layer):
        for t in range(3):
            w_in[3 * layer + t].wait()

        def chunk(i, carry):
            m, part = i // 4, i % 4
            at = pl.ds(pl.multiple_of(part * 64, 64), 64)
            to = pl.ds(pl.multiple_of(i * 64, 64), 64)
            a = wraw[layer, 3 * m, at, :]
            c = wraw[layer, 3 * m + 2, at, :]
            half = 0.5 * (a.astype(F32) + c.astype(F32))
            b = 0.5 * wraw[layer, 3 * m + 1, at, :].astype(F32)
            u1[layer - 1, 0, to, :] = a
            u1[layer - 1, 1, to, :] = (half + b).astype(BF16)
            u1[layer - 1, 2, to, :] = (half - b).astype(BF16)
            u1[layer - 1, 3, to, :] = c
            return carry
        lax.fori_loop(0, 36, chunk, 0)

    for t in range(3):
        weights_0(t)

    ahead = jnp.minimum(tms - 1 - tm, 1)
    beside = jnp.minimum(col, 1) + jnp.minimum(ncols - 1 - col, 1)
    pl.semaphore_wait(barrier, (1 + ahead) * 2 * (1 + beside) - 1)

    groups = [(0, 0, 4, 4), (1, 2, 2, 2), (1, 0, 2, 0)]

    def cell_copy(g, kind):
        dt, src, count, dst = groups[g]
        if kind == 0:
            s, d, dr, dc = cells.at[pl.ds(4 + src, count), pl.ds(1, 8)], cells.at[pl.ds(dst, count), pl.ds(1, 8)], 0, 0
        elif kind == 1:
            s, d, dr, dc = cells.at[pl.ds(4 + src, count), 8 - 7 * row], cells.at[pl.ds(dst, count), 9 * row], 1, 0
        else:
            side = kind % 2
            dc = 1 - 2 * side
            if kind < 4:
                s, d, dr = cell_stage.at[side, pl.ds(src, count)], cell_cols.at[side, pl.ds(dst, count)], 0
            else:
                s, d, dr = cell_tips.at[side, pl.ds(src, count)], cell_ends.at[side, pl.ds(dst, count)], 1
        copy = pltpu.make_async_remote_copy(
            src_ref=s, dst_ref=d, send_sem=c_send.at[g, kind], recv_sem=c_recv.at[g, kind],
            device_id=place(dt, dr, dc, 1), device_id_type=MESH)
        return copy, exists(dt, dc, 1), exists(dt, dc, -1)

    def cell_kinds(g):
        return range(1 if groups[g][0] == 0 else 0, 6)

    for g in range(3):
        for kind in cell_kinds(g):
            copy, there, _ = cell_copy(g, kind)
            when(there, copy.start)

    for copy in w_in[3:]:
        copy.start()

    def cells_arrived(g):
        for kind in cell_kinds(g):
            copy, _, there = cell_copy(g, kind)
            when(there, copy.wait_recv)

    fine = {1: (act1, cols1, ends1, stage1, tips1), 2: (act2, cols2, ends2, stage2, tips2)}

    def halo_copy(layer, pair, kind, dt=0):
        act, cols, ends, stage, tips = fine[layer]
        two = pl.ds(2 * pair, 2)
        to = pl.ds(0, 2) if dt else two
        if kind >= 5:
            f = kind - 5
            s, d, dr, dc = act.at[:, 2 * pair + f, pl.ds(1, 16)], act.at[:, f, pl.ds(1, 16)], 0, 0
        elif kind == 0:
            s, d, dr, dc = act.at[:, two, 16 - 15 * row], act.at[:, to, 17 * row], 1, 0
        else:
            side = (kind - 1) % 2
            dc = 1 - 2 * side
            if kind < 3:
                s, d, dr = stage.at[side, two], cols.at[side, to], 0
            else:
                s, d, dr = tips.at[side, two], ends.at[side, to], 1
        at = 0 if dt else pair
        copy = pltpu.make_async_remote_copy(
            src_ref=s, dst_ref=d, send_sem=h_send.at[layer - 1, at, kind], recv_sem=h_recv.at[layer - 1, at, kind],
            device_id=place(dt, dr, dc, 1), device_id_type=MESH)
        return copy, exists(dt, dc, 1), exists(dt, dc, -1)

    spatial = {(layer, pair): [(layer, pair, kind) for kind in range(5)] for layer, pair in ((1, 0), (1, 1), (1, 2), (2, 1), (2, 2))}
    onward = [(2, 2, kind, 1) for kind in (5, 6, 0, 1, 2, 3, 4)]

    def send(copies):
        for which in copies:
            copy, there, _ = halo_copy(*which)
            when(there, copy.start)

    def arrived(copies):
        for which in copies:
            copy, _, there = halo_copy(*which)
            when(there, copy.wait_recv)

    def put_edge(n, first, cols, ends, side, f):
        height = cols.shape[2]
        parted(cols[side, f].astype(F32), scr, n, pl.ds(first + 16, height, stride=16))
        end = ends[side, f]
        parted(jnp.where(row == 1, end, 0.0), scr, n, pl.ds(first, 1))
        parted(jnp.where(row == 0, end, 0.0), scr, n, pl.ds(first + 16 * height + 16, 1))

    def build_diffs(first, count):
        def frame(f, carry):
            c = cells[f].astype(F32).reshape(160, C)
            every = pl.ds(0, 160)
            parted(pltpu.roll(c, 1, 0), scr, 0, every)
            put_edge(0, 0, cell_cols, cell_ends, 0, f)
            parted(pltpu.roll(c, 159, 0), scr, 1, every)
            put_edge(1, 15, cell_cols, cell_ends, 1, f)
            for kx, x in enumerate((joined(scr, 0, every) - c, c, joined(scr, 1, every) - c)):
                mid = x[16:144]
                diffs[kx, f] = (x[0:128] - mid).astype(BF16)
                diffs[3 + kx, f] = mid.astype(BF16)
                diffs[6 + kx, f] = (x[32:160] - mid).astype(BF16)
            return carry
        lax.fori_loop(first, first + count, frame, 0)

    live = tm > 0

    def layer_0(pair):
        o = 2 * pair
        for m in range(9):
            lhs = jnp.concatenate([diffs[m, o + t:o + t + 2].reshape(256, C) for t in range(3)], axis=1)
            parted(jnp.dot(lhs, u0[m], preferred_element_type=F32), acc, m, pl.ds(0, 256))
        bias = bias_ref[0:1, :]

        def phases(at):
            p = [joined(acc, m, at) for m in range(9)]
            left, right = p[4] + p[3] + bias, p[4] + p[5] + bias
            out = [[left + (p[1] + p[0]), right + (p[1] + p[2])],
                   [left + (p[7] + p[6]), right + (p[7] + p[8])]]
            out = [[silu(v) for v in line] for line in out]
            if pair < 1:
                out = [[jnp.where(live, v, 0.0) for v in line] for line in out]
            return out

        for side, x in ((0, 15), (1, 0)):
            edge = phases(pl.ds(x, 16, stride=16))
            for py in range(2):
                parted(rounded(edge[py][1 - side]), scr, 0, pl.ds(py, 16, stride=2))
            for f in range(2):
                value = joined(scr, 0, pl.ds(16 * f, 16))
                stage1[side, o + f] = value.astype(BF16)
                tips1[side, o + f] = jnp.where(row == 0, value[15:16], value[0:1])
        for f in range(2):
            def line(i, carry, f=f):
                out = phases(pl.ds(pl.multiple_of(f * 128 + i * 16, 16), 16))
                for py in range(2):
                    for px in range(2):
                        act1[px, o + f, 1 + 2 * i + py] = out[py][px].astype(BF16)
                return carry
            lax.fori_loop(0, 8, line, 0, unroll=2)
        send(spatial[1, pair])

    def build_v(layer, pair):
        act, cols, ends, _, _ = fine[layer]
        v = v1 if layer == 1 else v2
        arrived(spatial[layer, pair] if (layer, pair) != (2, 0) else onward)
        for f in (2 * pair, 2 * pair + 1):
            e = act[0, f].astype(F32).reshape(288, C)
            o = act[1, f].astype(F32).reshape(288, C)
            every = pl.ds(0, 288)
            parted(pltpu.roll(o, 1, 0), scr, 0, every)
            put_edge(0, 0, cols, ends, 0, f)
            parted(pltpu.roll(e, 287, 0), scr, 1, every)
            put_edge(1, 15, cols, ends, 1, f)
            v[0, f] = (joined(scr, 0, every) - o).astype(BF16)
            v[1, f] = (e + o).astype(BF16)
            v[2, f] = (o - e).astype(BF16)
            v[3, f] = (e - joined(scr, 1, every)).astype(BF16)

    def products(layer, pair, times, more=False):
        v = v1 if layer == 1 else v2
        o = 2 * pair
        for k in range(4):
            lhs = jnp.concatenate(
                [v[k, o + t:o + t + 2, 16 * y:16 * y + 256].reshape(512, C) for t in times for y in range(3)], axis=1)
            weight = u1[layer - 1, k, 3 * C * times[0]:3 * C * (times[-1] + 1)]
            value = jnp.dot(lhs, weight, preferred_element_type=F32)
            every = pl.ds(0, 512)
            parted(value + joined(acc, k, every) if more else value, acc, k, every)

    def outputs(layer, at):
        bias = bias_ref[layer:layer + 1, :]
        m = [joined(acc, k, at) for k in range(4)]
        return (m[0] + m[1]) + (m[2] + bias), (m[1] - m[2]) - (m[3] - bias)

    def layer_1(pair):
        products(1, pair, (0, 1, 2))
        o = 2 * pair + 2

        def acted(at):
            return [silu(v) for v in outputs(1, at)]

        for side, x in ((0, 15), (1, 0)):
            value = rounded(acted(pl.ds(x, 32, stride=16))[1 - side])
            for f in range(2):
                line = value[16 * f:16 * f + 16]
                stage2[side, o + f] = line.astype(BF16)
                tips2[side, o + f] = jnp.where(row == 0, line[15:16], line[0:1])
        for f in range(2):
            def line(i, carry, f=f):
                e, o_ = acted(pl.ds(pl.multiple_of(f * 256 + i * 32, 32), 32))
                two = pl.ds(1 + 2 * i, 2)
                act2[0, o + f, two] = e.astype(BF16).reshape(2, 16, C)
                act2[1, o + f, two] = o_.astype(BF16).reshape(2, 16, C)
                return carry
            lax.fori_loop(0, 8, line, 0, unroll=2)
        send(spatial[2, pair + 1])

    def layer_2(pair):
        products(2, pair, (0, 1), more=True)
        for f in range(2):
            def line(i, carry, f=f):
                e, o_ = outputs(2, pl.ds(pl.multiple_of(f * 256 + i * 32, 32), 32))
                up = raw[2 * pair + f, pl.ds(pl.multiple_of(i * 16, 16), 16), :].astype(F32)
                up = jnp.concatenate([up, up], axis=0)
                for lane in range(2):
                    half = slice(128 * lane, 128 * lane + 128)
                    oscr[lane, pl.ds(0, 32, stride=2), :] = (up + e)[:, half]
                    oscr[lane, pl.ds(1, 32, stride=2), :] = (up + o_)[:, half]
                    obuf[2 * pair + f, pl.ds(pl.multiple_of(i * 64, 64), 64), half] = oscr[lane].astype(BF16)
                return carry
            lax.fori_loop(0, 8, line, 0)

    weights(1)
    weights(2)
    cells_arrived(0)
    build_diffs(4, 4)
    layer_0(2)
    cells_arrived(1)
    build_diffs(2, 2)
    layer_0(1)
    cells_arrived(2)
    build_diffs(0, 2)
    layer_0(0)
    build_v(1, 2)
    build_v(1, 1)
    layer_1(1)
    send(onward[:1])
    build_v(1, 0)
    layer_1(0)
    send(onward[1:])
    build_v(2, 2)
    products(2, 1, (2,))
    build_v(2, 1)
    layer_2(1)
    products(2, 0, (2,))
    build_v(2, 0)
    layer_2(0)

    for g in range(3):
        for kind in cell_kinds(g):
            copy, there, _ = cell_copy(g, kind)
            when(there, copy.wait_send)
    for which in [*sum(spatial.values(), []), *onward]:
        copy, there, _ = halo_copy(*which)
        when(there, copy.wait_send)


def solution(mesh):
    sizes = tuple(mesh.shape[name] for name in ("tm", "row", "col"))

    def local(coarse, kernels, biases):
        any_space = pl.BlockSpec(memory_space=pl.ANY)
        decoded = pl.pallas_call(
            functools.partial(kernel, sizes),
            out_shape=pltpu.VMEM((4, 512, C), BF16),
            in_specs=[any_space, any_space, pl.BlockSpec(memory_space=pltpu.VMEM)],
            out_specs=pl.BlockSpec(memory_space=pltpu.VMEM),
            scratch_shapes=[
                pltpu.VMEM((3, 27, C, C), BF16),
                pltpu.VMEM((9, 3 * C, C), BF16),
                pltpu.VMEM((2, 4, 9 * C, C), BF16),
                pltpu.VMEM((4, 128, C), BF16),
                pltpu.VMEM((8, 10, 16, C), BF16),
                pltpu.VMEM((2, 8, 8, C), BF16),
                pltpu.VMEM((2, 8, 1, C), F32),
                pltpu.VMEM((2, 4, 8, C), BF16),
                pltpu.VMEM((2, 4, 1, C), F32),
                pltpu.VMEM((9, 8, 128, C), BF16),
                pltpu.VMEM((2, 6, 18, 16, C), BF16),
                pltpu.VMEM((2, 6, 18, 16, C), BF16),
                pltpu.VMEM((2, 6, 16, C), BF16),
                pltpu.VMEM((2, 6, 16, C), BF16),
                pltpu.VMEM((2, 6, 1, C), F32),
                pltpu.VMEM((2, 6, 1, C), F32),
                pltpu.VMEM((2, 6, 16, C), BF16),
                pltpu.VMEM((2, 6, 16, C), BF16),
                pltpu.VMEM((2, 6, 1, C), F32),
                pltpu.VMEM((2, 6, 1, C), F32),
                pltpu.VMEM((4, 6, 288, C), BF16),
                pltpu.VMEM((4, 6, 288, C), BF16),
                pltpu.VMEM((9, 2, 512, 128), F32),
                pltpu.VMEM((2, 2, 288, 128), F32),
                pltpu.VMEM((2, 64, 128), F32),
                pltpu.SemaphoreType.DMA,
                pltpu.SemaphoreType.DMA((3, 3)),
                pltpu.SemaphoreType.DMA((3, 6)),
                pltpu.SemaphoreType.DMA((3, 6)),
                pltpu.SemaphoreType.DMA((2, 3, 7)),
                pltpu.SemaphoreType.DMA((2, 3, 7)),
            ],
            compiler_params=pltpu.CompilerParams(
                collective_id=0, has_side_effects=True, vmem_limit_bytes=56 * 2**20),
        )(coarse.reshape(4, 128, C), kernels.reshape(3, 27, C, C), biases)
        return decoded.reshape(4, 16, 32, C)

    return jax.shard_map(
        local, mesh=mesh, in_specs=(P("tm", "row", "col", None), P(), P()),
        out_specs=P("tm", "row", "col", None), check_vma=False)
```

```python
import functools

import jax
import jax.numpy as jnp
from jax import lax
from jax.experimental import pallas as pl
from jax.experimental.pallas import tpu as pltpu
from jax.sharding import PartitionSpec as P

F32 = jnp.float32
BF16 = jnp.bfloat16
MESH = pl.DeviceIdType.MESH
C = 256
TAP = 9


def silu(v):
    return v * (0.5 + 0.5 * jnp.tanh(0.5 * v))


def joined(ref, *at):
    *outer, rows = at
    return jnp.concatenate([ref[(*outer, half, rows)] for half in range(2)], axis=-1)


def parted(value, ref, *at):
    *outer, rows = at
    for half in range(2):
        ref[(*outer, half, rows)] = value[:, 128 * half:128 * half + 128]


def rounded(v):
    return v.astype(BF16).astype(F32)


def kernel(sizes, coarse_hbm, kernels_hbm, bias_ref, obuf,
           wraw, u0, u1, raw, cells, cell_cols, cell_ends, cell_stage, cell_tips, diffs,
           act1, act2, cols1, cols2, ends1, ends2, stage1, stage2, tips1, tips2, v1, v2, acc, scr, oscr,
           in_sem, w_sem, c_send, c_recv, h_send, h_recv):
    tms, rows, ncols = sizes
    tm, row, col = lax.axis_index("tm"), lax.axis_index("row"), lax.axis_index("col")
    other = 1 - row

    coarse_in = pltpu.make_async_copy(coarse_hbm, raw, in_sem)
    coarse_in.start()
    w_in = []
    for layer in range(3):
        for t in range(3):
            copy = pltpu.make_async_copy(
                kernels_hbm.at[layer, pl.ds(t * TAP, TAP)], wraw.at[layer, pl.ds(t * TAP, TAP)], w_sem.at[layer, t])
            w_in.append(copy)
    for copy in w_in[:3]:
        copy.start()

    peers = [(dt, dr, dc) for dt in range(2) for dr in range(2) for dc in (-1, 0, 1) if (dt, dr, dc) != (0, 0, 0)]

    def exists(dt, dc, sign):
        ok = True
        if dt:
            ok = (tm + sign * dt >= 0) & (tm + sign * dt < tms)
        if dc:
            near = (col + sign * dc >= 0) & (col + sign * dc < ncols)
            ok = near if ok is True else ok & near
        return ok

    def when(cond, body):
        if cond is True:
            body()
        else:
            pl.when(cond)(body)

    def place(dt, dr, dc, sign):
        return (tm + sign * dt, other if dr else row, col + sign * dc)

    barrier = pltpu.get_barrier_semaphore()
    for dt, dr, dc in peers:
        def greet(dt=dt, dr=dr, dc=dc):
            pl.semaphore_signal(barrier, inc=1, device_id=place(dt, dr, dc, -1), device_id_type=MESH)
        when(exists(dt, dc, -1), greet)

    def clear(*refs):
        for ref in refs:
            ref[...] = jnp.zeros(ref.shape, ref.dtype)

    clear(cells.at[:, 9 * row], act1.at[:, :, 17 * row], act2.at[:, :, 17 * row])
    for side, edge in ((0, 0), (1, ncols - 1)):
        @pl.when(col == edge)
        def _(side=side):
            clear(*(ref.at[side] for ref in (cell_cols, cell_ends, cols1, cols2, ends1, ends2)))

    def clear_frames(first, count):
        at = pl.ds(first, count)
        clear(cells.at[at], cell_cols.at[:, at], cell_ends.at[:, at])

    @pl.when(tm < 1)
    def _():
        clear_frames(0, 4)
        clear(act2.at[:, 0:2], cols2.at[:, 0:2], ends2.at[:, 0:2])

    coarse_in.wait()
    for f in range(4):
        acted = silu(raw[f].astype(F32)).astype(BF16)
        cells[4 + f, 1:9] = acted.reshape(8, 16, C)
        parted(acted.astype(F32), scr, 0, pl.ds(0, 128))
        for side, x in ((0, 15), (1, 0)):
            edge = joined(scr, 0, pl.ds(x, 8, stride=16))
            cell_stage[side, f] = edge.astype(BF16)
            cell_tips[side, f] = jnp.where(row == 0, edge[7:8], edge[0:1])

    def weights_0(t):
        w_in[t].wait()

        def chunk(i, carry):
            at = pl.ds(pl.multiple_of(i * 16, 16), 16)
            taps = [wraw[0, t * TAP + m, at, :].astype(F32) for m in range(9)]
            to = pl.ds(pl.multiple_of(t * C + i * 16, 16), 16)
            across = []
            for y in range(3):
                a, b, c = taps[3 * y:3 * y + 3]
                across.append([a, a + b + c, c])
            for kx in range(3):
                a, b, c = across[0][kx], across[1][kx], across[2][kx]
                for ky, value in enumerate((a, a + b + c, c)):
                    u0[ky * 3 + kx, to, :] = value.astype(BF16)
            return carry
        lax.fori_loop(0, 16, chunk, 0, unroll=2)

    def weights(layer):
        for t in range(3):
            w_in[3 * layer + t].wait()

        def chunk(i, carry):
            m, part = i // 4, i % 4
            at = pl.ds(pl.multiple_of(part * 64, 64), 64)
            to = pl.ds(pl.multiple_of(i * 64, 64), 64)
            half = 0.5 * (wraw[layer, 3 * m, at, :].astype(F32) + wraw[layer, 3 * m + 2, at, :].astype(F32))
            b = 0.5 * wraw[layer, 3 * m + 1, at, :].astype(F32)
            u1[layer - 1, 0, to, :] = (half + b).astype(BF16)
            u1[layer - 1, 1, to, :] = (half - b).astype(BF16)
            return carry
        lax.fori_loop(0, 36, chunk, 0, unroll=2)

    ahead = jnp.minimum(tms - 1 - tm, 1)
    beside = jnp.minimum(col, 1) + jnp.minimum(ncols - 1 - col, 1)
    pl.semaphore_wait(barrier, (1 + ahead) * 2 * (1 + beside) - 1)

    groups = [(0, 0, 4, 4), (1, 2, 2, 2), (1, 0, 2, 0)]

    def cell_copy(g, kind):
        dt, src, count, dst = groups[g]
        if kind == 0:
            s, d, dr, dc = cells.at[pl.ds(4 + src, count), pl.ds(1, 8)], cells.at[pl.ds(dst, count), pl.ds(1, 8)], 0, 0
        elif kind == 1:
            s, d, dr, dc = cells.at[pl.ds(4 + src, count), 8 - 7 * row], cells.at[pl.ds(dst, count), 9 * row], 1, 0
        else:
            side = kind % 2
            dc = 1 - 2 * side
            if kind < 4:
                s, d, dr = cell_stage.at[side, pl.ds(src, count)], cell_cols.at[side, pl.ds(dst, count)], 0
            else:
                s, d, dr = cell_tips.at[side, pl.ds(src, count)], cell_ends.at[side, pl.ds(dst, count)], 1
        copy = pltpu.make_async_remote_copy(
            src_ref=s, dst_ref=d, send_sem=c_send.at[g, kind], recv_sem=c_recv.at[g, kind],
            device_id=place(dt, dr, dc, 1), device_id_type=MESH)
        return copy, exists(dt, dc, 1), exists(dt, dc, -1)

    def cell_kinds(g):
        return range(1 if groups[g][0] == 0 else 0, 6)

    for g in range(3):
        for kind in cell_kinds(g):
            copy, there, _ = cell_copy(g, kind)
            when(there, copy.start)

    for copy in w_in[3:]:
        copy.start()

    def cells_arrived(g):
        for kind in cell_kinds(g):
            copy, _, there = cell_copy(g, kind)
            when(there, copy.wait_recv)

    fine = {1: (act1, cols1, ends1, stage1, tips1), 2: (act2, cols2, ends2, stage2, tips2)}

    def halo_copy(layer, pair, kind, dt=0):
        act, cols, ends, stage, tips = fine[layer]
        two = pl.ds(2 * pair, 2)
        to = pl.ds(0, 2) if dt else two
        if kind >= 5:
            f = kind - 5
            s, d, dr, dc = act.at[:, 2 * pair + f, pl.ds(1, 16)], act.at[:, f, pl.ds(1, 16)], 0, 0
        elif kind == 0:
            s, d, dr, dc = act.at[:, two, 16 - 15 * row], act.at[:, to, 17 * row], 1, 0
        else:
            side = (kind - 1) % 2
            dc = 1 - 2 * side
            if kind < 3:
                s, d, dr = stage.at[side, two], cols.at[side, to], 0
            else:
                s, d, dr = tips.at[side, two], ends.at[side, to], 1
        at = 0 if dt else pair
        copy = pltpu.make_async_remote_copy(
            src_ref=s, dst_ref=d, send_sem=h_send.at[layer - 1, at, kind], recv_sem=h_recv.at[layer - 1, at, kind],
            device_id=place(dt, dr, dc, 1), device_id_type=MESH)
        return copy, exists(dt, dc, 1), exists(dt, dc, -1)

    spatial = {(layer, pair): [(layer, pair, kind) for kind in range(5)] for layer, pair in ((1, 0), (1, 1), (1, 2), (2, 1), (2, 2))}
    onward = [(2, 2, kind, 1) for kind in (5, 6, 0, 1, 2, 3, 4)]

    def send(copies):
        for which in copies:
            copy, there, _ = halo_copy(*which)
            when(there, copy.start)

    def arrived(copies):
        for which in copies:
            copy, _, there = halo_copy(*which)
            when(there, copy.wait_recv)

    def put_edge(n, first, cols, ends, side, f):
        height = cols.shape[2]
        parted(cols[side, f].astype(F32), scr, n, pl.ds(first + 16, height, stride=16))
        end = ends[side, f]
        parted(jnp.where(row == 1, end, 0.0), scr, n, pl.ds(first, 1))
        parted(jnp.where(row == 0, end, 0.0), scr, n, pl.ds(first + 16 * height + 16, 1))

    def build_diffs(first, count):
        def frame(f, carry):
            c = cells[f].astype(F32).reshape(160, C)
            every = pl.ds(0, 160)
            parted(pltpu.roll(c, 1, 0), scr, 0, every)
            put_edge(0, 0, cell_cols, cell_ends, 0, f)
            parted(pltpu.roll(c, 159, 0), scr, 1, every)
            put_edge(1, 15, cell_cols, cell_ends, 1, f)
            for kx, x in enumerate((joined(scr, 0, every) - c, c, joined(scr, 1, every) - c)):
                mid = x[16:144]
                diffs[kx, f] = (x[0:128] - mid).astype(BF16)
                diffs[3 + kx, f] = mid.astype(BF16)
                diffs[6 + kx, f] = (x[32:160] - mid).astype(BF16)
            return carry
        for f in range(first, first + count):
            frame(f, 0)

    live = tm > 0

    def layer_0(pair):
        o = 2 * pair
        for m in range(9):
            lhs = jnp.concatenate([diffs[m, o + t:o + t + 2].reshape(256, C) for t in range(3)], axis=1)
            parted(jnp.dot(lhs, u0[m], preferred_element_type=F32), acc, m, pl.ds(0, 256))
        bias = bias_ref[0:1, :]

        def phases(at):
            p = [joined(acc, m, at) for m in range(9)]
            left, right = p[4] + p[3] + bias, p[4] + p[5] + bias
            out = [[left + (p[1] + p[0]), right + (p[1] + p[2])],
                   [left + (p[7] + p[6]), right + (p[7] + p[8])]]
            out = [[silu(v) for v in line] for line in out]
            if pair < 1:
                out = [[jnp.where(live, v, 0.0) for v in line] for line in out]
            return out

        for side, x in ((0, 15), (1, 0)):
            edge = phases(pl.ds(x, 16, stride=16))
            for py in range(2):
                parted(rounded(edge[py][1 - side]), scr, 0, pl.ds(py, 16, stride=2))
            for f in range(2):
                value = joined(scr, 0, pl.ds(16 * f, 16))
                stage1[side, o + f] = value.astype(BF16)
                tips1[side, o + f] = jnp.where(row == 0, value[15:16], value[0:1])
        for f in range(2):
            def line(i, carry, f=f):
                out = phases(pl.ds(f * 128 + i * 16, 16))
                for py in range(2):
                    for px in range(2):
                        act1[px, o + f, 1 + 2 * i + py] = out[py][px].astype(BF16)
                return carry
            for i in range(8):
                line(i, 0)
        send(spatial[1, pair])

    def build_v(layer, pair):
        act, cols, ends, _, _ = fine[layer]
        v = v1 if layer == 1 else v2
        arrived(spatial[layer, pair] if (layer, pair) != (2, 0) else onward)
        for f in (2 * pair, 2 * pair + 1):
            e = act[0, f].astype(F32).reshape(288, C)
            o = act[1, f].astype(F32).reshape(288, C)
            every = pl.ds(0, 288)
            parted(pltpu.roll(o, 1, 0), scr, 0, every)
            put_edge(0, 0, cols, ends, 0, f)
            parted(pltpu.roll(e, 287, 0), scr, 1, every)
            put_edge(1, 15, cols, ends, 1, f)
            v[0, f] = (joined(scr, 0, every) - o).astype(BF16)
            v[1, f] = (e + o).astype(BF16)
            v[2, f] = (o - e).astype(BF16)
            v[3, f] = (e - joined(scr, 1, every)).astype(BF16)

    def products(layer, pair, times, more=False):
        v = v1 if layer == 1 else v2
        o = 2 * pair
        for k in range(4):
            lhs = jnp.concatenate(
                [v[k, o + t:o + t + 2, 16 * y:16 * y + 256].reshape(512, C) for t in times for y in range(3)], axis=1)
            if k in (1, 2):
                weight = u1[layer - 1, k - 1, 3 * C * times[0]:3 * C * (times[-1] + 1)]
            else:
                weight = jnp.concatenate(
                    [wraw[layer, 3 * (3 * t + y) + 2 * (k // 3)] for t in times for y in range(3)], axis=0)
            value = jnp.dot(lhs, weight, preferred_element_type=F32)
            every = pl.ds(0, 512)
            parted(value + joined(acc, k, every) if more else value, acc, k, every)

    def outputs(layer, at):
        bias = bias_ref[layer:layer + 1, :]
        m = [joined(acc, k, at) for k in range(4)]
        return (m[0] + m[1]) + (m[2] + bias), (m[1] - m[2]) - (m[3] - bias)

    def layer_1(pair):
        products(1, pair, (0, 1, 2))
        o = 2 * pair + 2

        def acted(at):
            return [silu(v) for v in outputs(1, at)]

        for side, x in ((0, 15), (1, 0)):
            value = rounded(acted(pl.ds(x, 32, stride=16))[1 - side])
            for f in range(2):
                line = value[16 * f:16 * f + 16]
                stage2[side, o + f] = line.astype(BF16)
                tips2[side, o + f] = jnp.where(row == 0, line[15:16], line[0:1])
        for f in range(2):
            def line(i, carry, f=f):
                e, o_ = acted(pl.ds(f * 256 + i * 32, 32))
                two = pl.ds(1 + 2 * i, 2)
                act2[0, o + f, two] = e.astype(BF16).reshape(2, 16, C)
                act2[1, o + f, two] = o_.astype(BF16).reshape(2, 16, C)
                return carry
            for i in range(8):
                line(i, 0)
        send(spatial[2, pair + 1])

    def layer_2(pair):
        for f in range(2):
            def line(i, carry, f=f):
                e, o_ = outputs(2, pl.ds(f * 256 + i * 32, 32))
                up = raw[2 * pair + f, pl.ds(i * 16, 16), :].astype(F32)
                up = jnp.concatenate([up, up], axis=0)
                for lane in range(2):
                    half = slice(128 * lane, 128 * lane + 128)
                    oscr[i, lane, pl.ds(0, 32, stride=2), :] = (up + e)[:, half]
                    oscr[i, lane, pl.ds(1, 32, stride=2), :] = (up + o_)[:, half]
                    obuf[2 * pair + f, pl.ds(i * 64, 64), half] = oscr[i, lane].astype(BF16)
                return carry
            for i in range(8):
                line(i, 0)

    weights_0(0)
    weights_0(1)
    weights_0(2)
    weights(1)
    cells_arrived(0)
    build_diffs(4, 4)
    layer_0(2)
    cells_arrived(1)
    build_diffs(2, 2)
    layer_0(1)
    cells_arrived(2)
    build_diffs(0, 2)
    layer_0(0)
    build_v(1, 2)
    build_v(1, 1)
    layer_1(1)
    send(onward[:1])
    build_v(1, 0)
    layer_1(0)
    send(onward[1:])
    weights(2)
    build_v(2, 2)
    build_v(2, 1)
    products(2, 1, (0, 1, 2))
    layer_2(1)
    products(2, 0, (2,))
    build_v(2, 0)
    products(2, 0, (0, 1), more=True)
    layer_2(0)

    for g in range(3):
        for kind in cell_kinds(g):
            copy, there, _ = cell_copy(g, kind)
            when(there, copy.wait_send)
    for which in [*sum(spatial.values(), []), *onward]:
        copy, there, _ = halo_copy(*which)
        when(there, copy.wait_send)


def solution(mesh):
    sizes = tuple(mesh.shape[name] for name in ("tm", "row", "col"))

    def local(coarse, kernels, biases):
        any_space = pl.BlockSpec(memory_space=pl.ANY)
        decoded = pl.pallas_call(
            functools.partial(kernel, sizes),
            out_shape=pltpu.VMEM((4, 512, C), BF16),
            in_specs=[any_space, any_space, pl.BlockSpec(memory_space=pltpu.VMEM)],
            out_specs=pl.BlockSpec(memory_space=pltpu.VMEM),
            scratch_shapes=[
                pltpu.VMEM((3, 27, C, C), BF16),
                pltpu.VMEM((9, 3 * C, C), BF16),
                pltpu.VMEM((2, 2, 9 * C, C), BF16),
                pltpu.VMEM((4, 128, C), BF16),
                pltpu.VMEM((8, 10, 16, C), BF16),
                pltpu.VMEM((2, 8, 8, C), BF16),
                pltpu.VMEM((2, 8, 1, C), F32),
                pltpu.VMEM((2, 4, 8, C), BF16),
                pltpu.VMEM((2, 4, 1, C), F32),
                pltpu.VMEM((9, 8, 128, C), BF16),
                pltpu.VMEM((2, 6, 18, 16, C), BF16),
                pltpu.VMEM((2, 6, 18, 16, C), BF16),
                pltpu.VMEM((2, 6, 16, C), BF16),
                pltpu.VMEM((2, 6, 16, C), BF16),
                pltpu.VMEM((2, 6, 1, C), F32),
                pltpu.VMEM((2, 6, 1, C), F32),
                pltpu.VMEM((2, 6, 16, C), BF16),
                pltpu.VMEM((2, 6, 16, C), BF16),
                pltpu.VMEM((2, 6, 1, C), F32),
                pltpu.VMEM((2, 6, 1, C), F32),
                pltpu.VMEM((4, 6, 288, C), BF16),
                pltpu.VMEM((4, 6, 288, C), BF16),
                pltpu.VMEM((9, 2, 512, 128), F32),
                pltpu.VMEM((2, 2, 288, 128), F32),
                pltpu.VMEM((8, 2, 64, 128), F32),
                pltpu.SemaphoreType.DMA,
                pltpu.SemaphoreType.DMA((3, 3)),
                pltpu.SemaphoreType.DMA((3, 6)),
                pltpu.SemaphoreType.DMA((3, 6)),
                pltpu.SemaphoreType.DMA((2, 3, 7)),
                pltpu.SemaphoreType.DMA((2, 3, 7)),
            ],
            compiler_params=pltpu.CompilerParams(
                collective_id=0, has_side_effects=True, vmem_limit_bytes=56 * 2**20),
        )(coarse.reshape(4, 128, C), kernels.reshape(3, 27, C, C), biases)
        return decoded.reshape(4, 16, 32, C)

    return jax.shard_map(
        local, mesh=mesh, in_specs=(P("tm", "row", "col", None), P(), P()),
        out_specs=P("tm", "row", "col", None), check_vma=False)
```

```python
import functools

import jax
import jax.numpy as jnp
from jax import lax
from jax.experimental import pallas as pl
from jax.experimental.pallas import tpu as pltpu
from jax.sharding import PartitionSpec as P

F32 = jnp.float32
BF16 = jnp.bfloat16
MESH = pl.DeviceIdType.MESH
C = 256
TAP = 9


def silu(v):
    return v * (0.5 + 0.5 * jnp.tanh(0.5 * v))


def joined(ref, *at):
    *outer, rows = at
    return jnp.concatenate([ref[(*outer, half, rows)] for half in range(2)], axis=-1)


def parted(value, ref, *at):
    *outer, rows = at
    for half in range(2):
        ref[(*outer, half, rows)] = value[:, 128 * half:128 * half + 128]


def rounded(v):
    return v.astype(BF16).astype(F32)


def kernel(sizes, coarse_hbm, kernels_hbm, bias_ref, obuf,
           wraw, u0, u1, raw, cells, cell_cols, cell_ends, cell_stage, cell_tips, diffs,
           act1, act2, cols1, cols2, ends1, ends2, stage1, stage2, tips1, tips2, v1, v2, acc, scr, oscr,
           in_sem, w_sem, c_send, c_recv, h_send, h_recv):
    tms, rows, ncols = sizes
    tm, row, col = lax.axis_index("tm"), lax.axis_index("row"), lax.axis_index("col")
    other = 1 - row

    coarse_in = pltpu.make_async_copy(coarse_hbm, raw, in_sem)
    coarse_in.start()
    w_in = []
    for layer in range(3):
        for t in range(3):
            copy = pltpu.make_async_copy(
                kernels_hbm.at[layer, pl.ds(t * TAP, TAP)], wraw.at[layer, pl.ds(t * TAP, TAP)], w_sem.at[layer, t])
            w_in.append(copy)
    for copy in w_in[:3]:
        copy.start()

    peers = [(dt, dr, dc) for dt in range(2) for dr in range(2) for dc in (-1, 0, 1) if (dt, dr, dc) != (0, 0, 0)]

    def exists(dt, dc, sign):
        ok = True
        if dt:
            ok = (tm + sign * dt >= 0) & (tm + sign * dt < tms)
        if dc:
            near = (col + sign * dc >= 0) & (col + sign * dc < ncols)
            ok = near if ok is True else ok & near
        return ok

    def when(cond, body):
        if cond is True:
            body()
        else:
            pl.when(cond)(body)

    def place(dt, dr, dc, sign):
        return (tm + sign * dt, other if dr else row, col + sign * dc)

    barrier = pltpu.get_barrier_semaphore()
    for dt, dr, dc in peers:
        def greet(dt=dt, dr=dr, dc=dc):
            pl.semaphore_signal(barrier, inc=1, device_id=place(dt, dr, dc, -1), device_id_type=MESH)
        when(exists(dt, dc, -1), greet)

    def clear(*refs):
        for ref in refs:
            ref[...] = jnp.zeros(ref.shape, ref.dtype)

    clear(cells.at[:, 9 * row], act1.at[:, :, 17 * row], act2.at[:, :, 17 * row])
    for side, edge in ((0, 0), (1, ncols - 1)):
        @pl.when(col == edge)
        def _(side=side):
            clear(*(ref.at[side] for ref in (cell_cols, cell_ends, cols1, cols2, ends1, ends2)))

    def clear_frames(first, count):
        at = pl.ds(first, count)
        clear(cells.at[at], cell_cols.at[:, at], cell_ends.at[:, at])

    @pl.when(tm < 1)
    def _():
        clear_frames(0, 4)
        clear(act2.at[:, 0:2], cols2.at[:, 0:2], ends2.at[:, 0:2])

    coarse_in.wait()
    for f in range(4):
        acted = silu(raw[f].astype(F32)).astype(BF16)
        cells[4 + f, 1:9] = acted.reshape(8, 16, C)
        parted(acted.astype(F32), scr, 0, pl.ds(0, 128))
        for side, x in ((0, 15), (1, 0)):
            edge = joined(scr, 0, pl.ds(x, 8, stride=16))
            cell_stage[side, f] = edge.astype(BF16)
            cell_tips[side, f] = jnp.where(row == 0, edge[7:8], edge[0:1])

    def weights_0(t):
        w_in[t].wait()

        def chunk(i, carry):
            at = pl.ds(pl.multiple_of(i * 16, 16), 16)
            taps = [wraw[0, t * TAP + m, at, :].astype(F32) for m in range(9)]
            to = pl.ds(pl.multiple_of(t * C + i * 16, 16), 16)
            across = []
            for y in range(3):
                a, b, c = taps[3 * y:3 * y + 3]
                across.append([a, a + b + c, c])
            for kx in range(3):
                a, b, c = across[0][kx], across[1][kx], across[2][kx]
                for ky, value in enumerate((a, a + b + c, c)):
                    u0[ky * 3 + kx, to, :] = value.astype(BF16)
            return carry
        lax.fori_loop(0, 16, chunk, 0, unroll=2)

    def weights(layer):
        for t in range(3):
            w_in[3 * layer + t].wait()

        def chunk(i, carry):
            m, part = i // 4, i % 4
            at = pl.ds(pl.multiple_of(part * 64, 64), 64)
            to = pl.ds(pl.multiple_of(i * 64, 64), 64)
            half = 0.5 * (wraw[layer, 3 * m, at, :].astype(F32) + wraw[layer, 3 * m + 2, at, :].astype(F32))
            b = 0.5 * wraw[layer, 3 * m + 1, at, :].astype(F32)
            u1[layer - 1, 0, to, :] = (half + b).astype(BF16)
            u1[layer - 1, 1, to, :] = (half - b).astype(BF16)
            return carry
        lax.fori_loop(0, 36, chunk, 0, unroll=2)

    ahead = jnp.minimum(tms - 1 - tm, 1)
    beside = jnp.minimum(col, 1) + jnp.minimum(ncols - 1 - col, 1)
    pl.semaphore_wait(barrier, (1 + ahead) * 2 * (1 + beside) - 1)

    groups = [(0, 0, 4, 4), (1, 2, 2, 2), (1, 0, 2, 0)]

    def cell_copy(g, kind):
        dt, src, count, dst = groups[g]
        if kind == 0:
            s, d, dr, dc = cells.at[pl.ds(4 + src, count), pl.ds(1, 8)], cells.at[pl.ds(dst, count), pl.ds(1, 8)], 0, 0
        elif kind == 1:
            s, d, dr, dc = cells.at[pl.ds(4 + src, count), 8 - 7 * row], cells.at[pl.ds(dst, count), 9 * row], 1, 0
        else:
            side = kind % 2
            dc = 1 - 2 * side
            if kind < 4:
                s, d, dr = cell_stage.at[side, pl.ds(src, count)], cell_cols.at[side, pl.ds(dst, count)], 0
            else:
                s, d, dr = cell_tips.at[side, pl.ds(src, count)], cell_ends.at[side, pl.ds(dst, count)], 1
        copy = pltpu.make_async_remote_copy(
            src_ref=s, dst_ref=d, send_sem=c_send.at[g, kind], recv_sem=c_recv.at[g, kind],
            device_id=place(dt, dr, dc, 1), device_id_type=MESH)
        return copy, exists(dt, dc, 1), exists(dt, dc, -1)

    def cell_kinds(g):
        return range(1 if groups[g][0] == 0 else 0, 6)

    for g in range(3):
        for kind in cell_kinds(g):
            copy, there, _ = cell_copy(g, kind)
            when(there, copy.start)

    for copy in w_in[3:]:
        copy.start()

    def cells_arrived(g):
        for kind in cell_kinds(g):
            copy, _, there = cell_copy(g, kind)
            when(there, copy.wait_recv)

    fine = {1: (act1, cols1, ends1, stage1, tips1), 2: (act2, cols2, ends2, stage2, tips2)}

    def halo_copy(layer, pair, kind, dt=0):
        act, cols, ends, stage, tips = fine[layer]
        two = pl.ds(2 * pair, 2)
        to = pl.ds(0, 2) if dt else two
        if kind >= 5:
            f = kind - 5
            s, d, dr, dc = act.at[:, 2 * pair + f, pl.ds(1, 16)], act.at[:, f, pl.ds(1, 16)], 0, 0
        elif kind == 0:
            s, d, dr, dc = act.at[:, two, 16 - 15 * row], act.at[:, to, 17 * row], 1, 0
        else:
            side = (kind - 1) % 2
            dc = 1 - 2 * side
            if kind < 3:
                s, d, dr = stage.at[side, two], cols.at[side, to], 0
            else:
                s, d, dr = tips.at[side, two], ends.at[side, to], 1
        at = 0 if dt else pair
        copy = pltpu.make_async_remote_copy(
            src_ref=s, dst_ref=d, send_sem=h_send.at[layer - 1, at, kind], recv_sem=h_recv.at[layer - 1, at, kind],
            device_id=place(dt, dr, dc, 1), device_id_type=MESH)
        return copy, exists(dt, dc, 1), exists(dt, dc, -1)

    spatial = {(layer, pair): [(layer, pair, kind) for kind in range(5)] for layer, pair in ((1, 0), (1, 1), (1, 2), (2, 1), (2, 2))}
    onward = [(2, 2, kind, 1) for kind in (5, 0, 1, 2, 3, 4, 6)]

    def send(copies):
        for which in copies:
            copy, there, _ = halo_copy(*which)
            when(there, copy.start)

    def arrived(copies):
        for which in copies:
            copy, _, there = halo_copy(*which)
            when(there, copy.wait_recv)

    def put_edge(n, first, cols, ends, side, f):
        height = cols.shape[2]
        parted(cols[side, f].astype(F32), scr, n, pl.ds(first + 16, height, stride=16))
        end = ends[side, f]
        parted(jnp.where(row == 1, end, 0.0), scr, n, pl.ds(first, 1))
        parted(jnp.where(row == 0, end, 0.0), scr, n, pl.ds(first + 16 * height + 16, 1))

    def build_diffs(first, count):
        def frame(f, carry):
            c = cells[f].astype(F32).reshape(160, C)
            every = pl.ds(0, 160)
            parted(pltpu.roll(c, 1, 0), scr, 0, every)
            put_edge(0, 0, cell_cols, cell_ends, 0, f)
            parted(pltpu.roll(c, 159, 0), scr, 1, every)
            put_edge(1, 15, cell_cols, cell_ends, 1, f)
            for kx, x in enumerate((joined(scr, 0, every) - c, c, joined(scr, 1, every) - c)):
                mid = x[16:144]
                diffs[kx, f] = (x[0:128] - mid).astype(BF16)
                diffs[3 + kx, f] = mid.astype(BF16)
                diffs[6 + kx, f] = (x[32:160] - mid).astype(BF16)
            return carry
        for f in range(first, first + count):
            frame(f, 0)

    live = tm > 0

    def layer_0(pair):
        o = 2 * pair
        for m in range(9):
            lhs = jnp.concatenate([diffs[m, o + t:o + t + 2].reshape(256, C) for t in range(3)], axis=1)
            parted(jnp.dot(lhs, u0[m], preferred_element_type=F32), acc, m, pl.ds(0, 256))
        bias = bias_ref[0:1, :]

        def phases(at):
            p = [joined(acc, m, at) for m in range(9)]
            left, right = p[4] + p[3] + bias, p[4] + p[5] + bias
            out = [[left + (p[1] + p[0]), right + (p[1] + p[2])],
                   [left + (p[7] + p[6]), right + (p[7] + p[8])]]
            out = [[silu(v) for v in line] for line in out]
            if pair < 1:
                out = [[jnp.where(live, v, 0.0) for v in line] for line in out]
            return out

        for side, x in ((0, 15), (1, 0)):
            edge = phases(pl.ds(x, 16, stride=16))
            for py in range(2):
                parted(rounded(edge[py][1 - side]), scr, 0, pl.ds(py, 16, stride=2))
            for f in range(2):
                value = joined(scr, 0, pl.ds(16 * f, 16))
                stage1[side, o + f] = value.astype(BF16)
                tips1[side, o + f] = jnp.where(row == 0, value[15:16], value[0:1])
        for f in range(2):
            def line(i, carry, f=f):
                out = phases(pl.ds(f * 128 + i * 16, 16))
                for py in range(2):
                    for px in range(2):
                        act1[px, o + f, 1 + 2 * i + py] = out[py][px].astype(BF16)
                return carry
            for i in range(8):
                line(i, 0)
        send(spatial[1, pair])

    def build_v(layer, pair, frames=(0, 1)):
        act, cols, ends, _, _ = fine[layer]
        v = v1 if layer == 1 else v2
        if (layer, pair) != (2, 0):
            arrived(spatial[layer, pair])
        else:
            arrived(onward[:6] if 0 in frames else onward[6:])
        for f in (2 * pair + f for f in frames):
            e = act[0, f].astype(F32).reshape(288, C)
            o = act[1, f].astype(F32).reshape(288, C)
            every = pl.ds(0, 288)
            parted(pltpu.roll(o, 1, 0), scr, 0, every)
            put_edge(0, 0, cols, ends, 0, f)
            parted(pltpu.roll(e, 287, 0), scr, 1, every)
            put_edge(1, 15, cols, ends, 1, f)
            v[0, f] = (joined(scr, 0, every) - o).astype(BF16)
            v[1, f] = (e + o).astype(BF16)
            v[2, f] = (o - e).astype(BF16)
            v[3, f] = (e - joined(scr, 1, every)).astype(BF16)

    def products(layer, pair, times, more=False, frames=(0, 1)):
        v = v1 if layer == 1 else v2
        o, first, rows_ = 2 * pair, frames[0], 256 * len(frames)
        for k in range(4):
            lhs = jnp.concatenate(
                [v[k, o + t + first:o + t + first + len(frames), 16 * y:16 * y + 256].reshape(rows_, C)
                 for t in times for y in range(3)], axis=1)
            if k in (1, 2):
                weight = u1[layer - 1, k - 1, 3 * C * times[0]:3 * C * (times[-1] + 1)]
            else:
                weight = jnp.concatenate(
                    [wraw[layer, 3 * (3 * t + y) + 2 * (k // 3)] for t in times for y in range(3)], axis=0)
            value = jnp.dot(lhs, weight, preferred_element_type=F32)
            every = pl.ds(256 * first, rows_)
            parted(value + joined(acc, k, every) if more else value, acc, k, every)

    def outputs(layer, at):
        bias = bias_ref[layer:layer + 1, :]
        m = [joined(acc, k, at) for k in range(4)]
        return (m[0] + m[1]) + (m[2] + bias), (m[1] - m[2]) - (m[3] - bias)

    def layer_1(pair):
        o = 2 * pair + 2

        def acted(at):
            return [silu(v) for v in outputs(1, at)]

        for side, x in ((0, 15), (1, 0)):
            value = rounded(acted(pl.ds(x, 32, stride=16))[1 - side])
            for f in range(2):
                line = value[16 * f:16 * f + 16]
                stage2[side, o + f] = line.astype(BF16)
                tips2[side, o + f] = jnp.where(row == 0, line[15:16], line[0:1])
        for f in range(2):
            def line(i, carry, f=f):
                e, o_ = acted(pl.ds(f * 256 + i * 32, 32))
                two = pl.ds(1 + 2 * i, 2)
                act2[0, o + f, two] = e.astype(BF16).reshape(2, 16, C)
                act2[1, o + f, two] = o_.astype(BF16).reshape(2, 16, C)
                return carry
            for i in range(8):
                line(i, 0)
        send(spatial[2, pair + 1])

    def layer_2(pair):
        for f in range(2):
            def line(i, carry, f=f):
                e, o_ = outputs(2, pl.ds(f * 256 + i * 32, 32))
                up = raw[2 * pair + f, pl.ds(i * 16, 16), :].astype(F32)
                up = jnp.concatenate([up, up], axis=0)
                for lane in range(2):
                    half = slice(128 * lane, 128 * lane + 128)
                    oscr[i, lane, pl.ds(0, 32, stride=2), :] = (up + e)[:, half]
                    oscr[i, lane, pl.ds(1, 32, stride=2), :] = (up + o_)[:, half]
                    obuf[2 * pair + f, pl.ds(i * 64, 64), half] = oscr[i, lane].astype(BF16)
                return carry
            for i in range(8):
                line(i, 0)

    weights_0(0)
    weights_0(1)
    weights_0(2)
    weights(1)
    cells_arrived(0)
    build_diffs(4, 4)
    layer_0(2)
    weights(2)
    cells_arrived(1)
    build_diffs(2, 2)
    layer_0(1)
    cells_arrived(2)
    build_diffs(0, 2)
    layer_0(0)
    build_v(1, 2)
    products(1, 1, (2,))
    build_v(1, 1)
    products(1, 1, (0, 1), more=True)
    layer_1(1)
    send(onward[:6])
    build_v(1, 0)
    products(1, 0, (0, 1, 2))
    layer_1(0)
    send(onward[6:])
    build_v(2, 2)
    products(2, 1, (2,))
    build_v(2, 1)
    products(2, 1, (0, 1), more=True)
    layer_2(1)
    products(2, 0, (2,), frames=(0,))
    products(2, 0, (1, 2), frames=(1,))
    build_v(2, 0, (0,))
    products(2, 0, (0,), more=True, frames=(0,))
    build_v(2, 0, (1,))
    products(2, 0, (1,), more=True, frames=(0,))
    products(2, 0, (0,), more=True, frames=(1,))
    layer_2(0)

    for g in range(3):
        for kind in cell_kinds(g):
            copy, there, _ = cell_copy(g, kind)
            when(there, copy.wait_send)
    for which in [*sum(spatial.values(), []), *onward]:
        copy, there, _ = halo_copy(*which)
        when(there, copy.wait_send)


def solution(mesh):
    sizes = tuple(mesh.shape[name] for name in ("tm", "row", "col"))

    def local(coarse, kernels, biases):
        any_space = pl.BlockSpec(memory_space=pl.ANY)
        decoded = pl.pallas_call(
            functools.partial(kernel, sizes),
            out_shape=pltpu.VMEM((4, 512, C), BF16),
            in_specs=[any_space, any_space, pl.BlockSpec(memory_space=pltpu.VMEM)],
            out_specs=pl.BlockSpec(memory_space=pltpu.VMEM),
            scratch_shapes=[
                pltpu.VMEM((3, 27, C, C), BF16),
                pltpu.VMEM((9, 3 * C, C), BF16),
                pltpu.VMEM((2, 2, 9 * C, C), BF16),
                pltpu.VMEM((4, 128, C), BF16),
                pltpu.VMEM((8, 10, 16, C), BF16),
                pltpu.VMEM((2, 8, 8, C), BF16),
                pltpu.VMEM((2, 8, 1, C), F32),
                pltpu.VMEM((2, 4, 8, C), BF16),
                pltpu.VMEM((2, 4, 1, C), F32),
                pltpu.VMEM((9, 8, 128, C), BF16),
                pltpu.VMEM((2, 6, 18, 16, C), BF16),
                pltpu.VMEM((2, 6, 18, 16, C), BF16),
                pltpu.VMEM((2, 6, 16, C), BF16),
                pltpu.VMEM((2, 6, 16, C), BF16),
                pltpu.VMEM((2, 6, 1, C), F32),
                pltpu.VMEM((2, 6, 1, C), F32),
                pltpu.VMEM((2, 6, 16, C), BF16),
                pltpu.VMEM((2, 6, 16, C), BF16),
                pltpu.VMEM((2, 6, 1, C), F32),
                pltpu.VMEM((2, 6, 1, C), F32),
                pltpu.VMEM((4, 6, 288, C), BF16),
                pltpu.VMEM((4, 6, 288, C), BF16),
                pltpu.VMEM((9, 2, 512, 128), F32),
                pltpu.VMEM((2, 2, 288, 128), F32),
                pltpu.VMEM((8, 2, 64, 128), F32),
                pltpu.SemaphoreType.DMA,
                pltpu.SemaphoreType.DMA((3, 3)),
                pltpu.SemaphoreType.DMA((3, 6)),
                pltpu.SemaphoreType.DMA((3, 6)),
                pltpu.SemaphoreType.DMA((2, 3, 7)),
                pltpu.SemaphoreType.DMA((2, 3, 7)),
            ],
            compiler_params=pltpu.CompilerParams(
                collective_id=0, has_side_effects=True, vmem_limit_bytes=56 * 2**20),
        )(coarse.reshape(4, 128, C), kernels.reshape(3, 27, C, C), biases)
        return decoded.reshape(4, 16, 32, C)

    return jax.shard_map(
        local, mesh=mesh, in_specs=(P("tm", "row", "col", None), P(), P()),
        out_specs=P("tm", "row", "col", None), check_vma=False)
```

```python
import functools

import jax
import jax.numpy as jnp
from jax import lax
from jax.experimental import pallas as pl
from jax.experimental.pallas import tpu as pltpu
from jax.sharding import PartitionSpec as P

F32 = jnp.float32
BF16 = jnp.bfloat16
MESH = pl.DeviceIdType.MESH
C = 256
TAP = 9


def silu(v):
    return v * (0.5 + 0.5 * jnp.tanh(0.5 * v))


def joined(ref, *at):
    *outer, rows = at
    return jnp.concatenate([ref[(*outer, half, rows)] for half in range(2)], axis=-1)


def parted(value, ref, *at):
    *outer, rows = at
    for half in range(2):
        ref[(*outer, half, rows)] = value[:, 128 * half:128 * half + 128]


def rounded(v):
    return v.astype(BF16).astype(F32)


def kernel(sizes, coarse_hbm, kernels_hbm, bias_ref, obuf,
           wraw, u0, u1, raw, cells, cell_cols, cell_ends, cell_stage, cell_tips, diffs,
           act1, act2, cols1, cols2, ends1, ends2, stage1, stage2, tips1, tips2, v1, v2, acc, scr, oscr,
           in_sem, w_sem, c_send, c_recv, h_send, h_recv):
    tms, rows, ncols = sizes
    tm, row, col = lax.axis_index("tm"), lax.axis_index("row"), lax.axis_index("col")
    other = 1 - row

    coarse_in = pltpu.make_async_copy(coarse_hbm, raw, in_sem)
    coarse_in.start()
    w_in = []
    for layer in range(3):
        for t in range(3):
            copy = pltpu.make_async_copy(
                kernels_hbm.at[layer, pl.ds(t * TAP, TAP)], wraw.at[layer, pl.ds(t * TAP, TAP)], w_sem.at[layer, t])
            w_in.append(copy)
    for copy in w_in[:3]:
        copy.start()

    peers = [(dt, dr, dc) for dt in range(2) for dr in range(2) for dc in (-1, 0, 1) if (dt, dr, dc) != (0, 0, 0)]

    def exists(dt, dc, sign):
        ok = True
        if dt:
            ok = (tm + sign * dt >= 0) & (tm + sign * dt < tms)
        if dc:
            near = (col + sign * dc >= 0) & (col + sign * dc < ncols)
            ok = near if ok is True else ok & near
        return ok

    def when(cond, body):
        if cond is True:
            body()
        else:
            pl.when(cond)(body)

    def place(dt, dr, dc, sign):
        return (tm + sign * dt, other if dr else row, col + sign * dc)

    barrier = pltpu.get_barrier_semaphore()
    for dt, dr, dc in peers:
        def greet(dt=dt, dr=dr, dc=dc):
            pl.semaphore_signal(barrier, inc=1, device_id=place(dt, dr, dc, -1), device_id_type=MESH)
        when(exists(dt, dc, -1), greet)

    def clear(*refs):
        for ref in refs:
            ref[...] = jnp.zeros(ref.shape, ref.dtype)

    clear(cells.at[:, 9 * row], act1.at[:, :, 17 * row], act2.at[:, :, 17 * row])
    for side, edge in ((0, 0), (1, ncols - 1)):
        @pl.when(col == edge)
        def _(side=side):
            clear(*(ref.at[side] for ref in (cell_cols, cell_ends, cols1, cols2, ends1, ends2)))

    def clear_frames(first, count):
        at = pl.ds(first, count)
        clear(cells.at[at], cell_cols.at[:, at], cell_ends.at[:, at])

    @pl.when(tm < 1)
    def _():
        clear_frames(0, 4)
        clear(act2.at[:, 0:2], cols2.at[:, 0:2], ends2.at[:, 0:2])

    coarse_in.wait()
    for f in range(4):
        acted = silu(raw[f].astype(F32)).astype(BF16)
        cells[4 + f, 1:9] = acted.reshape(8, 16, C)
        parted(acted.astype(F32), scr, f, pl.ds(0, 128))
        for side, x in ((0, 15), (1, 0)):
            edge = joined(scr, f, pl.ds(x, 8, stride=16))
            cell_stage[side, f] = edge.astype(BF16)
            cell_tips[side, f] = jnp.where(row == 0, edge[7:8], edge[0:1])

    def weights_0(t):
        w_in[t].wait()

        def chunk(i, carry):
            at = pl.ds(pl.multiple_of(i * 16, 16), 16)
            taps = [wraw[0, t * TAP + m, at, :].astype(F32) for m in range(9)]
            to = pl.ds(pl.multiple_of(t * C + i * 16, 16), 16)
            across = []
            for y in range(3):
                a, b, c = taps[3 * y:3 * y + 3]
                across.append([a, a + b + c, c])
            for kx in range(3):
                a, b, c = across[0][kx], across[1][kx], across[2][kx]
                for ky, value in enumerate((a, a + b + c, c)):
                    u0[ky * 3 + kx, to, :] = value.astype(BF16)
            return carry
        lax.fori_loop(0, 16, chunk, 0, unroll=2)

    def weights(layer):
        for t in range(3):
            w_in[3 * layer + t].wait()

        def chunk(i, carry):
            m, part = i // 4, i % 4
            at = pl.ds(pl.multiple_of(part * 64, 64), 64)
            to = pl.ds(pl.multiple_of(i * 64, 64), 64)
            half = 0.5 * (wraw[layer, 3 * m, at, :].astype(F32) + wraw[layer, 3 * m + 2, at, :].astype(F32))
            b = 0.5 * wraw[layer, 3 * m + 1, at, :].astype(F32)
            u1[layer - 1, 0, to, :] = (half + b).astype(BF16)
            u1[layer - 1, 1, to, :] = (half - b).astype(BF16)
            return carry
        lax.fori_loop(0, 36, chunk, 0, unroll=2)

    ahead = jnp.minimum(tms - 1 - tm, 1)
    beside = jnp.minimum(col, 1) + jnp.minimum(ncols - 1 - col, 1)
    pl.semaphore_wait(barrier, (1 + ahead) * 2 * (1 + beside) - 1)

    groups = [(0, 0, 4, 4), (1, 2, 2, 2), (1, 0, 2, 0)]

    def cell_copy(g, kind):
        dt, src, count, dst = groups[g]
        if kind == 0:
            s, d, dr, dc = cells.at[pl.ds(4 + src, count), pl.ds(1, 8)], cells.at[pl.ds(dst, count), pl.ds(1, 8)], 0, 0
        elif kind == 1:
            s, d, dr, dc = cells.at[pl.ds(4 + src, count), 8 - 7 * row], cells.at[pl.ds(dst, count), 9 * row], 1, 0
        else:
            side = kind % 2
            dc = 1 - 2 * side
            if kind < 4:
                s, d, dr = cell_stage.at[side, pl.ds(src, count)], cell_cols.at[side, pl.ds(dst, count)], 0
            else:
                s, d, dr = cell_tips.at[side, pl.ds(src, count)], cell_ends.at[side, pl.ds(dst, count)], 1
        copy = pltpu.make_async_remote_copy(
            src_ref=s, dst_ref=d, send_sem=c_send.at[g, kind], recv_sem=c_recv.at[g, kind],
            device_id=place(dt, dr, dc, 1), device_id_type=MESH)
        return copy, exists(dt, dc, 1), exists(dt, dc, -1)

    def cell_kinds(g):
        return range(1 if groups[g][0] == 0 else 0, 6)

    for g in range(3):
        for kind in cell_kinds(g):
            copy, there, _ = cell_copy(g, kind)
            when(there, copy.start)

    for copy in w_in[3:]:
        copy.start()

    def cells_arrived(g):
        for kind in cell_kinds(g):
            copy, _, there = cell_copy(g, kind)
            when(there, copy.wait_recv)

    fine = {1: (act1, cols1, ends1, stage1, tips1), 2: (act2, cols2, ends2, stage2, tips2)}

    def halo_copy(layer, pair, kind, dt=0):
        act, cols, ends, stage, tips = fine[layer]
        two = pl.ds(2 * pair, 2)
        to = pl.ds(0, 2) if dt else two
        if kind >= 5:
            f = kind - 5
            s, d, dr, dc = act.at[:, 2 * pair + f, pl.ds(1, 16)], act.at[:, f, pl.ds(1, 16)], 0, 0
        elif kind == 0:
            s, d, dr, dc = act.at[:, two, 16 - 15 * row], act.at[:, to, 17 * row], 1, 0
        else:
            side = (kind - 1) % 2
            dc = 1 - 2 * side
            if kind < 3:
                s, d, dr = stage.at[side, two], cols.at[side, to], 0
            else:
                s, d, dr = tips.at[side, two], ends.at[side, to], 1
        at = 0 if dt else pair
        copy = pltpu.make_async_remote_copy(
            src_ref=s, dst_ref=d, send_sem=h_send.at[layer - 1, at, kind], recv_sem=h_recv.at[layer - 1, at, kind],
            device_id=place(dt, dr, dc, 1), device_id_type=MESH)
        return copy, exists(dt, dc, 1), exists(dt, dc, -1)

    spatial = {(layer, pair): [(layer, pair, kind) for kind in range(5)] for layer, pair in ((1, 0), (1, 1), (1, 2), (2, 1), (2, 2))}
    onward = [(2, 2, kind, 1) for kind in (5, 0, 1, 2, 3, 4, 6)]

    def send(copies):
        for which in copies:
            copy, there, _ = halo_copy(*which)
            when(there, copy.start)

    def arrived(copies):
        for which in copies:
            copy, _, there = halo_copy(*which)
            when(there, copy.wait_recv)

    def put_edge(n, first, cols, ends, side, f):
        height = cols.shape[2]
        parted(cols[side, f].astype(F32), scr, n, pl.ds(first + 16, height, stride=16))
        end = ends[side, f]
        parted(jnp.where(row == 1, end, 0.0), scr, n, pl.ds(first, 1))
        parted(jnp.where(row == 0, end, 0.0), scr, n, pl.ds(first + 16 * height + 16, 1))

    def build_diffs(first, count):
        def frame(f, carry):
            c = cells[f].astype(F32).reshape(160, C)
            every, n = pl.ds(0, 160), 2 * (f % 2)
            parted(pltpu.roll(c, 1, 0), scr, n, every)
            put_edge(n, 0, cell_cols, cell_ends, 0, f)
            parted(pltpu.roll(c, 159, 0), scr, n + 1, every)
            put_edge(n + 1, 15, cell_cols, cell_ends, 1, f)
            for kx, x in enumerate((joined(scr, n, every) - c, c, joined(scr, n + 1, every) - c)):
                mid = x[16:144]
                diffs[kx, f] = (x[0:128] - mid).astype(BF16)
                diffs[3 + kx, f] = mid.astype(BF16)
                diffs[6 + kx, f] = (x[32:160] - mid).astype(BF16)
            return carry
        for f in range(first, first + count):
            frame(f, 0)

    live = tm > 0

    def layer_0(pair):
        o = 2 * pair
        for m in range(9):
            lhs = jnp.concatenate([diffs[m, o + t:o + t + 2].reshape(256, C) for t in range(3)], axis=1)
            parted(jnp.dot(lhs, u0[m], preferred_element_type=F32), acc, m, pl.ds(0, 256))
        bias = bias_ref[0:1, :]

        def phases(at):
            p = [joined(acc, m, at) for m in range(9)]
            left, right = p[4] + p[3] + bias, p[4] + p[5] + bias
            out = [[left + (p[1] + p[0]), right + (p[1] + p[2])],
                   [left + (p[7] + p[6]), right + (p[7] + p[8])]]
            out = [[silu(v) for v in line] for line in out]
            if pair < 1:
                out = [[jnp.where(live, v, 0.0) for v in line] for line in out]
            return out

        for side, x in ((0, 15), (1, 0)):
            edge = phases(pl.ds(x, 16, stride=16))
            for py in range(2):
                parted(rounded(edge[py][1 - side]), scr, side, pl.ds(py, 16, stride=2))
            for f in range(2):
                value = joined(scr, side, pl.ds(16 * f, 16))
                stage1[side, o + f] = value.astype(BF16)
                tips1[side, o + f] = jnp.where(row == 0, value[15:16], value[0:1])
        for f in range(2):
            def line(i, carry, f=f):
                out = phases(pl.ds(f * 128 + i * 16, 16))
                for py in range(2):
                    for px in range(2):
                        act1[px, o + f, 1 + 2 * i + py] = out[py][px].astype(BF16)
                return carry
            for i in range(8):
                line(i, 0)
        send(spatial[1, pair])

    def build_v(layer, pair, frames=(0, 1)):
        act, cols, ends, _, _ = fine[layer]
        v = v1 if layer == 1 else v2
        if (layer, pair) != (2, 0):
            arrived(spatial[layer, pair])
        else:
            arrived(onward[:6] if 0 in frames else onward[6:])
        for f in (2 * pair + f for f in frames):
            e = act[0, f].astype(F32).reshape(288, C)
            o = act[1, f].astype(F32).reshape(288, C)
            every, n = pl.ds(0, 288), 2 * (f % 2)
            parted(pltpu.roll(o, 1, 0), scr, n, every)
            put_edge(n, 0, cols, ends, 0, f)
            parted(pltpu.roll(e, 287, 0), scr, n + 1, every)
            put_edge(n + 1, 15, cols, ends, 1, f)
            v[0, f] = (joined(scr, n, every) - o).astype(BF16)
            v[1, f] = (e + o).astype(BF16)
            v[2, f] = (o - e).astype(BF16)
            v[3, f] = (e - joined(scr, n + 1, every)).astype(BF16)

    def products(layer, pair, times, more=False, frames=(0, 1)):
        v = v1 if layer == 1 else v2
        o, first, rows_ = 2 * pair, frames[0], 256 * len(frames)
        for k in range(4):
            lhs = jnp.concatenate(
                [v[k, o + t + first:o + t + first + len(frames), 16 * y:16 * y + 256].reshape(rows_, C)
                 for t in times for y in range(3)], axis=1)
            if k in (1, 2):
                weight = u1[layer - 1, k - 1, 3 * C * times[0]:3 * C * (times[-1] + 1)]
            else:
                weight = jnp.concatenate(
                    [wraw[layer, 3 * (3 * t + y) + 2 * (k // 3)] for t in times for y in range(3)], axis=0)
            value = jnp.dot(lhs, weight, preferred_element_type=F32)
            every = pl.ds(256 * first, rows_)
            parted(value + joined(acc, k, every) if more else value, acc, k, every)

    def outputs(layer, at):
        bias = bias_ref[layer:layer + 1, :]
        m = [joined(acc, k, at) for k in range(4)]
        return (m[0] + m[1]) + (m[2] + bias), (m[1] - m[2]) - (m[3] - bias)

    def layer_1(pair):
        o = 2 * pair + 2

        def acted(at):
            return [silu(v) for v in outputs(1, at)]

        for side, x in ((0, 15), (1, 0)):
            value = rounded(acted(pl.ds(x, 32, stride=16))[1 - side])
            for f in range(2):
                line = value[16 * f:16 * f + 16]
                stage2[side, o + f] = line.astype(BF16)
                tips2[side, o + f] = jnp.where(row == 0, line[15:16], line[0:1])
        for f in range(2):
            def line(i, carry, f=f):
                e, o_ = acted(pl.ds(f * 256 + i * 32, 32))
                two = pl.ds(1 + 2 * i, 2)
                act2[0, o + f, two] = e.astype(BF16).reshape(2, 16, C)
                act2[1, o + f, two] = o_.astype(BF16).reshape(2, 16, C)
                return carry
            for i in range(8):
                line(i, 0)
        send(spatial[2, pair + 1])

    def layer_2(pair):
        for f in range(2):
            def line(i, carry, f=f):
                e, o_ = outputs(2, pl.ds(f * 256 + i * 32, 32))
                up = raw[2 * pair + f, pl.ds(i * 16, 16), :].astype(F32)
                up = jnp.concatenate([up, up], axis=0)
                for lane in range(2):
                    half = slice(128 * lane, 128 * lane + 128)
                    oscr[i, lane, pl.ds(0, 32, stride=2), :] = (up + e)[:, half]
                    oscr[i, lane, pl.ds(1, 32, stride=2), :] = (up + o_)[:, half]
                    obuf[2 * pair + f, pl.ds(i * 64, 64), half] = oscr[i, lane].astype(BF16)
                return carry
            for i in range(8):
                line(i, 0)

    weights_0(0)
    weights_0(1)
    weights_0(2)
    weights(1)
    cells_arrived(0)
    build_diffs(4, 4)
    layer_0(2)
    weights(2)
    cells_arrived(1)
    build_diffs(2, 2)
    layer_0(1)
    cells_arrived(2)
    build_diffs(0, 2)
    layer_0(0)
    build_v(1, 2)
    products(1, 1, (2,))
    build_v(1, 1)
    products(1, 1, (0, 1), more=True)
    layer_1(1)
    send(onward[:6])
    build_v(1, 0)
    products(1, 0, (0, 1, 2))
    layer_1(0)
    send(onward[6:])
    build_v(2, 2)
    products(2, 1, (2,))
    build_v(2, 1)
    products(2, 1, (0, 1), more=True)
    layer_2(1)
    products(2, 0, (2,), frames=(0,))
    products(2, 0, (1, 2), frames=(1,))
    build_v(2, 0, (0,))
    products(2, 0, (0,), more=True, frames=(0,))
    build_v(2, 0, (1,))
    products(2, 0, (1,), more=True, frames=(0,))
    products(2, 0, (0,), more=True, frames=(1,))
    layer_2(0)

    for g in range(3):
        for kind in cell_kinds(g):
            copy, there, _ = cell_copy(g, kind)
            when(there, copy.wait_send)
    for which in [*sum(spatial.values(), []), *onward]:
        copy, there, _ = halo_copy(*which)
        when(there, copy.wait_send)


def solution(mesh):
    sizes = tuple(mesh.shape[name] for name in ("tm", "row", "col"))

    def local(coarse, kernels, biases):
        any_space = pl.BlockSpec(memory_space=pl.ANY)
        decoded = pl.pallas_call(
            functools.partial(kernel, sizes),
            out_shape=pltpu.VMEM((4, 512, C), BF16),
            in_specs=[any_space, any_space, pl.BlockSpec(memory_space=pltpu.VMEM)],
            out_specs=pl.BlockSpec(memory_space=pltpu.VMEM),
            scratch_shapes=[
                pltpu.VMEM((3, 27, C, C), BF16),
                pltpu.VMEM((9, 3 * C, C), BF16),
                pltpu.VMEM((2, 2, 9 * C, C), BF16),
                pltpu.VMEM((4, 128, C), BF16),
                pltpu.VMEM((8, 10, 16, C), BF16),
                pltpu.VMEM((2, 8, 8, C), BF16),
                pltpu.VMEM((2, 8, 1, C), F32),
                pltpu.VMEM((2, 4, 8, C), BF16),
                pltpu.VMEM((2, 4, 1, C), F32),
                pltpu.VMEM((9, 8, 128, C), BF16),
                pltpu.VMEM((2, 6, 18, 16, C), BF16),
                pltpu.VMEM((2, 6, 18, 16, C), BF16),
                pltpu.VMEM((2, 6, 16, C), BF16),
                pltpu.VMEM((2, 6, 16, C), BF16),
                pltpu.VMEM((2, 6, 1, C), F32),
                pltpu.VMEM((2, 6, 1, C), F32),
                pltpu.VMEM((2, 6, 16, C), BF16),
                pltpu.VMEM((2, 6, 16, C), BF16),
                pltpu.VMEM((2, 6, 1, C), F32),
                pltpu.VMEM((2, 6, 1, C), F32),
                pltpu.VMEM((4, 6, 288, C), BF16),
                pltpu.VMEM((4, 6, 288, C), BF16),
                pltpu.VMEM((9, 2, 512, 128), F32),
                pltpu.VMEM((4, 2, 288, 128), F32),
                pltpu.VMEM((8, 2, 64, 128), F32),
                pltpu.SemaphoreType.DMA,
                pltpu.SemaphoreType.DMA((3, 3)),
                pltpu.SemaphoreType.DMA((3, 6)),
                pltpu.SemaphoreType.DMA((3, 6)),
                pltpu.SemaphoreType.DMA((2, 3, 7)),
                pltpu.SemaphoreType.DMA((2, 3, 7)),
            ],
            compiler_params=pltpu.CompilerParams(
                collective_id=0, has_side_effects=True, vmem_limit_bytes=56 * 2**20),
        )(coarse.reshape(4, 128, C), kernels.reshape(3, 27, C, C), biases)
        return decoded.reshape(4, 16, 32, C)

    return jax.shard_map(
        local, mesh=mesh, in_specs=(P("tm", "row", "col", None), P(), P()),
        out_specs=P("tm", "row", "col", None), check_vma=False)
```
